32 devices in a mesh: groups: 2 (over y), tm: 16 (over z, x, core).
Axes of the slice: x: 2, y: 2, z: 4, core: 2. Of those that a mesh axis runs over, the one named last changes fastest.
Arguments:
- frames: bfloat16 [4096, 8192], P('tm', 'groups'), parts along dimension 1, may hold values from -6 to 6
- frame_valid: int32 [8192], P(('groups', 'tm')), parts along dimension 0, may hold values 0 or 1
- valid_count: int32 [32], P('groups'), parts along dimension 0, may hold values from 32 to 128, as said below
- block_map: int32 [32, 256], P('groups'), parts along dimension 0, may hold values from 0 to 255, as said below
- offsets: int32 [4, 2], replicated, may hold values from -4 to 4
Outputs:
- cross: float32 [512, 4, 2, 2048], P(('groups', 'tm')), parts along dimension 0
The draws below stay inside these ranges and needn't reach their ends.
There are 2 independent parts, one for each index of `groups`. The reference program is written for one: setup_inputs(seed, part) draws one part's arguments, and reference() takes and returns one part's arrays. A program takes and returns all parts, laid end to end along the dimension named above; an argument that names none is the same for every part. Nothing has to cross between parts.
Inputs may be any that keep to these rules, and one draw needn't show every extreme that they name: `valid_count`: at most half of a tile's pixels are valid. Some tile has exactly 128 valid pixels and another exactly 32 in every draw; the others are spread evenly between the two. `block_map`: each row is a permutation of the pixels of a tile. Row steps lie in -4 to 4.
All inputs are finite; a program needn't handle non-finite values. No bound on the sum of `frame_valid` on one device may be relied on, other than what follows from the above.
Results may differ from the reference program's by a relative error of at most 0.0052.
Values may be sent and summed in bfloat16 or wider, within the bound.
No kernel may reach another device: no remote copies, remote signals or barrier semaphores. Data moves between devices by JAX's collectives and lax.ppermute only.
A program may use at most 64 MiB of HBM per device.

```python
import math
import jax
import jax.numpy as jnp
from jax import lax

ROWS = 16
FRAMES = 4096
BAND = 256
REACH = 4
TILES = 16
TILE_PIX = 256
PIX = 4096


def draw_valid_count(key, part):
    spread = jax.random.randint(jax.random.fold_in(key, 11), (TILES,), TILE_PIX // 8, TILE_PIX // 2 + 1)
    fullest = jax.random.randint(jax.random.fold_in(key, 12), (), 0, TILES)
    step = jax.random.randint(jax.random.fold_in(key, 13), (), 1, TILES)
    emptiest = (fullest + step) % TILES
    tile_idx = jnp.arange(TILES)
    counts = jnp.where(tile_idx == fullest, TILE_PIX // 2, spread)
    counts = jnp.where(tile_idx == emptiest, TILE_PIX // 8, counts)
    return counts.astype(jnp.int32)


def draw_block_map(key, part):
    tile_keys = jax.random.split(jax.random.fold_in(key, 21), TILES)
    return jax.vmap(lambda single: jax.random.permutation(single, TILE_PIX))(tile_keys).astype(jnp.int32)


def draw_offsets(key, part):
    row_steps = jax.random.randint(jax.random.fold_in(key, 31), (4,), -REACH, REACH + 1)
    second = jax.random.randint(jax.random.fold_in(key, 32), (), 1, REACH + 1)
    fourth = jax.random.randint(jax.random.fold_in(key, 33), (), -REACH, 0)
    col_steps = jnp.stack([jnp.int32(REACH), second.astype(jnp.int32), jnp.int32(-REACH), fourth.astype(jnp.int32)])
    return jnp.stack([row_steps.astype(jnp.int32), col_steps], axis=1).astype(jnp.int32)


def with_ends(drawn, rng, least, high):
    longest = drawn.shape.index(max(drawn.shape))
    spots = []
    for shift in (0, 1):
        where = [jax.random.randint(jax.random.fold_in(rng, axis), (), 0, length) for axis, length in enumerate(drawn.shape)]
        where[longest] = (where[longest] + shift) % drawn.shape[longest]
        spots.append(tuple(where))
    return drawn.at[spots[0]].set(least).at[spots[1]].set(high)


def steps_of(key, dims, cuts, low, largest):
    level, own = 1.0, jax.random.fold_in(key, 6)
    for axis_at, parts in cuts:
        draws = jnp.exp(jax.random.uniform(jax.random.fold_in(own, axis_at), (parts,), jnp.float32, low / len(cuts), largest / len(cuts)))
        level = level * jnp.repeat(draws, dims[axis_at] // parts).reshape([-1 if axis == axis_at else 1 for axis in range(len(dims))])
    return level


def centred(rng, dims, width, bound, pieces=(), kind=jnp.bfloat16):
    entries = jax.random.normal(rng, dims, jnp.float32) * width
    if len(pieces) > 0:
        entries = steps_of(rng, dims, pieces, -0.22, 0.18) * entries
    return jnp.clip(entries, min=-bound, max=bound).astype(kind)


def setup_inputs(seed: int = 0, part: int = 0) -> dict:
    key_list = jax.random.split(jax.random.key(seed), 6)
    own_keys = jax.random.split(jax.random.fold_in(key_list[5], part), 6)
    return {
        "frames": centred(own_keys[0], (FRAMES, PIX), 1.0, 6.0, ((0, 16),)),
        "frame_valid": with_ends((jax.random.randint(own_keys[1], (FRAMES,), 0, 8) < 7).astype(jnp.int32), jax.random.fold_in(own_keys[1], 1), 0, 1),
        "valid_count": draw_valid_count(jax.random.fold_in(jax.random.fold_in(key_list[5], part), 71), part),
        "block_map": draw_block_map(jax.random.fold_in(jax.random.fold_in(key_list[5], part), 71), part),
        "offsets": draw_offsets(jax.random.fold_in(key_list[5], 71), part),
    }


def table_piece(frames_len, bin_start, band_width):
    frame_idx = jnp.arange(frames_len, dtype=jnp.int32)[:, None]
    bin_idx = bin_start + jnp.arange(band_width, dtype=jnp.int32)[None, :]
    angles = (frame_idx * bin_idx % frames_len).astype(jnp.float32) * (2.0 * math.pi / frames_len)
    scaling = 1.0 / math.sqrt(frames_len)
    return (jnp.concatenate([jnp.cos(angles), -jnp.sin(angles)], axis=1) * scaling).astype(jnp.bfloat16)

def validity(valid_count, block_map):
    tile_count, tile_pix = block_map.shape
    slot_idx = jnp.arange(tile_pix, dtype=jnp.int32)[None, :]
    live = (slot_idx < valid_count[:, None]).astype(jnp.float32)
    tile_idx = jnp.arange(tile_count, dtype=jnp.int32)[:, None]
    return jnp.zeros((tile_count, tile_pix), jnp.float32).at[tile_idx, block_map].set(live)

def cross_block(extended, ext_valid, offsets, tile_width):
    spectra = extended.astype(jnp.float32)
    row_count = spectra.shape[0]
    half = spectra.shape[2] // 2
    padded = jnp.pad(spectra, ((REACH, REACH), (0, 0), (0, 0)))
    padded_valid = jnp.pad(ext_valid, ((REACH, REACH), (0, 0)))
    own_spec = spectra[:, REACH:REACH + tile_width]
    own_valid = ext_valid[:, REACH:REACH + tile_width]
    own_real = own_spec[..., :half]
    own_imag = own_spec[..., half:]
    results = []
    for which in range(offsets.shape[0]):
        row_step = offsets[which, 0] + REACH
        col_step = offsets[which, 1] + REACH
        shifted = lax.dynamic_slice(padded, (row_step, col_step, jnp.int32(0)), (row_count, tile_width, 2 * half))
        shifted_valid = lax.dynamic_slice(padded_valid, (row_step, col_step), (row_count, tile_width))
        other_real = shifted[..., :half]
        other_imag = shifted[..., half:]
        real_part = lax.optimization_barrier(jnp.sum(own_real * other_real + own_imag * other_imag, axis=0))
        imag_part = lax.optimization_barrier(jnp.sum(own_imag * other_real - own_real * other_imag, axis=0))
        pair_count = lax.optimization_barrier(jnp.sum(own_valid * shifted_valid, axis=0))
        scaling = 1.0 / jnp.maximum(pair_count, 1.0)
        results.append(jnp.stack([real_part, imag_part], axis=1) * scaling[:, None, None])
    return jnp.stack(results, axis=1)

def reference(frames, frame_valid, valid_count, block_map, offsets):
    frames_len, pixel_count = frames.shape
    masked = (frames * frame_valid[:, None].astype(frames.dtype)).astype(jnp.float32)
    valid_all = validity(valid_count, block_map)
    tile_count, tile_pix = valid_all.shape
    tile_width = tile_pix // ROWS
    col_count = tile_count * tile_width
    valid_grid = valid_all.reshape(tile_count, ROWS, tile_width).transpose(1, 0, 2).reshape(ROWS, col_count)
    ext_valid = jnp.pad(valid_grid, ((0, 0), (REACH, REACH)))
    pixel_valid = valid_all.reshape(pixel_count)

    def one_band(band_index):
        bin_start = (band_index * BAND).astype(jnp.int32)
        table = table_piece(frames_len, bin_start, BAND).astype(jnp.float32)
        spectra = lax.dot_general(masked, table, (((0,), (0,)), ((), ())), precision=lax.Precision.HIGHEST)
        spectra = (spectra * pixel_valid[:, None]).astype(jnp.bfloat16)
        spectra = spectra.reshape(tile_count, ROWS, tile_width, 2 * BAND).transpose(1, 0, 2, 3)
        spectra = spectra.reshape(ROWS, col_count, 2 * BAND)
        extended = jnp.pad(spectra, ((0, 0), (REACH, REACH), (0, 0)))
        return cross_block(extended, ext_valid, offsets, col_count)
    results = lax.map(one_band, jnp.arange(frames_len // 2 // BAND, dtype=jnp.int32))
    return results.transpose(1, 2, 3, 0, 4).reshape(col_count, offsets.shape[0], 2, frames_len // 2)
```

```python
import functools
import math

import jax
import jax.numpy as jnp
import numpy as np
from jax import lax
from jax.experimental import pallas as pl
from jax.experimental.pallas import tpu as pltpu
from jax.sharding import PartitionSpec as P

ROWS = 16
REACH = 4
RADIX = 16
LANES = 128


def dft_tables(frames_len):
    inner = frames_len // RADIX
    steps = np.arange(inner)
    angles = 2.0 * np.pi * (np.outer(steps, steps) % inner) / inner
    table = np.concatenate([np.cos(angles), -np.sin(angles)], axis=1) / math.sqrt(frames_len)
    turns = 2.0 * np.pi * np.outer(np.arange(RADIX), steps) / frames_len
    twiddle = np.stack([np.cos(turns), -np.sin(turns)], axis=1)
    twiddle = np.broadcast_to(twiddle[:, :, None, :], (RADIX, 2, 8, inner))
    return jnp.asarray(table, jnp.bfloat16), jnp.asarray(twiddle, jnp.float32)


def compact_kernel(count_ref, valid_ref, map_ref, frames_ref, out_ref):
    step = pl.program_id(0)
    batch, frame_dev, slots = out_ref.shape
    tile_pix = frames_ref.shape[1] // batch
    per_phase = frame_dev // RADIX
    row = lax.broadcasted_iota(jnp.int32, (frame_dev, frame_dev), 0)
    col = lax.broadcasted_iota(jnp.int32, (frame_dev, frame_dev), 1)
    source = row % per_phase * RADIX + row // per_phase
    keep = jnp.broadcast_to(valid_ref[...], (frame_dev, frame_dev))
    order = jnp.where(col == source, keep, 0).astype(jnp.float32).astype(jnp.bfloat16)
    pixel = lax.broadcasted_iota(jnp.int32, (tile_pix, slots), 0)
    slot = lax.broadcasted_iota(jnp.int32, (tile_pix, slots), 1)
    for pair in range(batch // 2):
        parts = []
        for which in (2 * pair, 2 * pair + 1):
            count = count_ref[step * batch + which]
            held = jnp.broadcast_to(map_ref[0, which : which + 1, :slots], (tile_pix, slots))
            hot = jnp.where((held == pixel) & (slot < count), 1.0, 0.0).astype(jnp.bfloat16)
            block = frames_ref[:, which * tile_pix : (which + 1) * tile_pix]
            parts.append(jnp.dot(block, hot, preferred_element_type=jnp.float32))
        both = jnp.concatenate(parts, axis=1).astype(jnp.bfloat16)
        both = jnp.dot(order, both, preferred_element_type=jnp.float32).astype(jnp.bfloat16)
        out_ref[2 * pair] = both[:, :slots]
        out_ref[2 * pair + 1] = both[:, slots:]


def compact(frames, frame_valid, valid_count, block_map):
    frame_dev, pixel_count = frames.shape
    tile_count, tile_pix = block_map.shape
    slots = tile_pix // 2
    batch = 4
    return pl.pallas_call(
        compact_kernel,
        name="compact",
        grid=(tile_count // batch,),
        out_shape=jax.ShapeDtypeStruct((tile_count, frame_dev, slots), jnp.bfloat16),
        in_specs=[
            pl.BlockSpec(memory_space=pltpu.SMEM),
            pl.BlockSpec((1, frame_dev), lambda i: (0, 0)),
            pl.BlockSpec((1, batch, tile_pix), lambda i: (i, 0, 0)),
            pl.BlockSpec((frame_dev, batch * tile_pix), lambda i: (0, i)),
        ],
        out_specs=pl.BlockSpec((batch, frame_dev, slots), lambda i: (i, 0, 0)),
    )(
        valid_count,
        frame_valid.reshape(1, frame_dev),
        block_map.reshape(tile_count // batch, batch, tile_pix),
        frames,
    )


def rotate(real, imag, cos, sin):
    return real * cos - imag * sin, real * sin + imag * cos


def four_point(values):
    (r0, i0), (r1, i1), (r2, i2), (r3, i3) = values
    er, ei, fr, fi = r0 + r2, i0 + i2, r0 - r2, i0 - i2
    gr, gi, hr, hi = r1 + r3, i1 + i3, r1 - r3, i1 - i3
    return [(er + gr, ei + gi), (fr + hi, fi - hr), (er - gr, ei - gi), (fr - hi, fi + hr)]


def sixteen_point_low(values):
    inner = [four_point([values[4 * n + m] for n in range(4)]) for m in range(4)]
    low = [None] * 8
    for k in range(4):
        parts = []
        for m in range(4):
            real, imag = inner[m][k]
            turn = m * k % 16
            if turn == 0:
                parts.append((real, imag))
            elif turn == 4:
                parts.append((imag, -real))
            else:
                angle = -2.0 * math.pi * turn / 16
                parts.append(rotate(real, imag, math.cos(angle), math.sin(angle)))
        (r0, i0), (r1, i1), (r2, i2), (r3, i3) = parts
        low[k] = ((r0 + r2) + (r1 + r3), (i0 + i2) + (i1 + i3))
        low[k + 4] = ((r0 - r2) + (i1 - i3), (i0 - i2) - (r1 - r3))
    return low


def transform_kernel(place_ref, frames_ref, table_ref, twiddle_ref, own_ref, left_ref, right_ref, phases, spread):
    slots = own_ref.shape[0]
    rows = own_ref.shape[1]
    half = rows // 2
    inner = table_ref.shape[0]
    width = place_ref.shape[0] // (ROWS + 2 * REACH)
    for phase in range(RADIX):
        if len(frames_ref.shape) == 3:
            per_phase = frames_ref.shape[1] // RADIX
            block = frames_ref[:, phase * per_phase : (phase + 1) * per_phase, :].reshape(inner, slots)
        else:
            block = frames_ref[phase].reshape(inner, slots)
        phases[phase] = lax.dot_general(
            block, table_ref[...], (((0,), (0,)), ((), ())), preferred_element_type=jnp.float32
        )
    chunks = inner // LANES

    def one_group(group, carry):
        first = pl.multiple_of(group * 8, 8)
        for chunk in range(chunks):
            lanes = pl.ds(chunk * LANES, LANES)
            values = []
            for phase in range(RADIX):
                real = phases[phase, pl.ds(first, 8), lanes]
                imag = phases[phase, pl.ds(first, 8), pl.ds(inner + chunk * LANES, LANES)]
                if phase > 0:
                    real, imag = rotate(real, imag, twiddle_ref[phase, 0, :, lanes], twiddle_ref[phase, 1, :, lanes])
                values.append((real, imag))
            for high, (real, imag) in enumerate(sixteen_point_low(values)):
                at = first * rows + high * chunks + chunk
                spread[pl.ds(at, 8, stride=rows), :] = real
                spread[pl.ds(at + half, 8, stride=rows), :] = imag
        return carry

    lax.fori_loop(0, slots // 8, one_group, 0)

    def one_slot(slot, carry):
        at = pl.multiple_of(slot * rows, rows)
        own_ref[slot] = spread[pl.ds(at, rows), :].astype(jnp.bfloat16)
        return carry

    lax.fori_loop(0, slots, one_slot, 0, unroll=4)
    spread[pl.ds(slots * rows, rows), :] = jnp.zeros((rows, LANES), jnp.float32)

    def one_edge(spot, carry):
        row = spot // REACH
        column = spot % REACH
        base = (row + REACH) * width + REACH + column
        slot = jnp.minimum(place_ref[base], slots)
        left_ref[spot] = spread[pl.ds(pl.multiple_of(slot * rows, rows), rows), :].astype(jnp.bfloat16)
        slot = jnp.minimum(place_ref[base + width - 3 * REACH], slots)
        right_ref[spot] = spread[pl.ds(pl.multiple_of(slot * rows, rows), rows), :].astype(jnp.bfloat16)
        return carry

    lax.fori_loop(0, ROWS * REACH, one_edge, 0, unroll=4)


def transform(place, tile_frames, slots, frames_len):
    table, twiddle = dft_tables(frames_len)
    inner = frames_len // RADIX
    rows = frames_len // LANES
    edge = ROWS * REACH
    whole = pl.BlockSpec(memory_space=pltpu.VMEM)
    return pl.pallas_call(
        transform_kernel,
        name="transform",
        out_shape=(
            jax.ShapeDtypeStruct((slots, rows, LANES), jnp.bfloat16),
            jax.ShapeDtypeStruct((edge, rows, LANES), jnp.bfloat16),
            jax.ShapeDtypeStruct((edge, rows, LANES), jnp.bfloat16),
        ),
        in_specs=[pl.BlockSpec(memory_space=pltpu.SMEM), whole, whole, whole],
        out_specs=(whole, whole, whole),
        scratch_shapes=[
            pltpu.VMEM((RADIX, slots, 2 * inner), jnp.float32),
            pltpu.VMEM(((slots + 1) * rows, LANES), jnp.float32),
        ],
    )(place, tile_frames, table, twiddle)


def cross_kernel(place_ref, offset_ref, map_ref, count_ref, own_hbm, right_hbm, left_hbm, out_ref, held, total, pairs, sem):
    slots, rows, _ = own_hbm.shape
    half = rows // 2
    edge = ROWS * REACH
    width = place_ref.shape[0] // (ROWS + 2 * REACH)
    tile_width = width - 2 * REACH
    empty = slots + 2 * edge
    copies = [
        pltpu.make_async_copy(own_hbm, held.at[pl.ds(0, slots)], sem.at[0]),
        pltpu.make_async_copy(right_hbm, held.at[pl.ds(slots, edge)], sem.at[1]),
        pltpu.make_async_copy(left_hbm, held.at[pl.ds(slots + edge, edge)], sem.at[2]),
    ]
    for copy in copies:
        copy.start()
    columns = total.shape[0]
    held[empty] = jnp.zeros((rows, LANES), jnp.bfloat16)

    def clear(spot, carry):
        total[spot] = jnp.zeros((rows, LANES), jnp.float32)
        pairs[spot] = 0
        return carry

    lax.fori_loop(0, columns, clear, 0)
    for copy in copies:
        copy.wait()
    offsets = offset_ref.shape[0]
    shifts = [offset_ref[j, 0] * width + offset_ref[j, 1] for j in range(offsets)]

    def one_slot(slot, carry):
        pixel = map_ref[slot]
        row = pixel // tile_width
        column = pixel % tile_width
        base = (row + REACH) * width + REACH + column
        own_real = held[slot, :half].astype(jnp.float32)
        own_imag = held[slot, half:].astype(jnp.float32)
        for j in range(offsets):
            other = place_ref[base + shifts[j]]
            at = column * offsets + j
            pairs[at] = pairs[at] + jnp.where(other < empty, 1, 0)
            real = held[other, :half].astype(jnp.float32)
            imag = held[other, half:].astype(jnp.float32)
            total[at, :half] += own_real * real + own_imag * imag
            total[at, half:] += own_imag * real - own_real * imag
        return carry

    lax.fori_loop(0, count_ref[0], one_slot, 0)

    def finish(spot, carry):
        seen = jnp.full((1, LANES), pairs[spot], jnp.int32).astype(jnp.float32)
        scaling = 1.0 / jnp.maximum(seen, 1.0)
        out_ref[spot, pl.ds(0, half, stride=2), :] = total[spot, :half] * scaling
        out_ref[spot, pl.ds(1, half, stride=2), :] = total[spot, half:] * scaling
        return carry

    lax.fori_loop(0, columns, finish, 0)


def cross(place, offsets, own_map, own_count, own, from_right, from_left, tile_width):
    slots, rows, _ = own.shape
    spots = tile_width * offsets.shape[0]
    small = pl.BlockSpec(memory_space=pltpu.SMEM)
    large = pl.BlockSpec(memory_space=pl.ANY)
    return pl.pallas_call(
        cross_kernel,
        name="cross",
        out_shape=jax.ShapeDtypeStruct((spots, rows, LANES), jnp.float32),
        in_specs=[small, small, small, small, large, large, large],
        out_specs=pl.BlockSpec(memory_space=pltpu.VMEM),
        scratch_shapes=[
            pltpu.VMEM((slots + 2 * ROWS * REACH + 1, rows, LANES), jnp.bfloat16),
            pltpu.VMEM((spots, rows, LANES), jnp.float32),
            pltpu.SMEM((spots,), jnp.int32),
            pltpu.SemaphoreType.DMA((3,)),
        ],
    )(place, offsets, own_map, own_count, own, from_right, from_left)


def neighbour_places(valid_count, block_map, position):
    tile_pix = block_map.shape[1]
    slots = tile_pix // 2
    tile_width = tile_pix // ROWS
    edge = ROWS * REACH
    empty = slots + 2 * edge
    padded_count = jnp.pad(valid_count, ((1, 1),))
    padded_map = jnp.pad(block_map, ((1, 1), (0, 0)))
    counts = lax.dynamic_slice_in_dim(padded_count, position, 3, 0)
    maps = lax.dynamic_slice_in_dim(padded_map, position, 3, 0)[:, :slots]
    slot_idx = jnp.arange(slots, dtype=jnp.int32)
    pixel_idx = jnp.arange(tile_pix, dtype=jnp.int32)
    match = (maps[:, :, None] == pixel_idx[None, None, :]) & (slot_idx[None, :, None] < counts[:, None, None])
    found = jnp.max(jnp.where(match, slot_idx[None, :, None], -1), axis=1)
    grid = found.reshape(3, ROWS, tile_width)
    spot = (jnp.arange(ROWS, dtype=jnp.int32) * REACH)[:, None] + jnp.arange(REACH, dtype=jnp.int32)[None, :]
    own = jnp.where(grid[1] >= 0, grid[1], empty)
    right = jnp.where(grid[2][:, :REACH] >= 0, slots + spot, empty)
    left = jnp.where(grid[0][:, tile_width - REACH :] >= 0, slots + edge + spot, empty)
    place = jnp.concatenate([left, own, right], axis=1)
    place = jnp.pad(place, ((REACH, REACH), (0, 0)), constant_values=empty)
    return place.reshape(-1), maps[1], counts[1:2]


def per_device(frames, frame_valid, valid_count, block_map, offsets):
    devices = lax.axis_size("tm")
    position = lax.axis_index("tm")
    frame_dev = frames.shape[0]
    frames_len = frame_dev * devices
    tile_pix = block_map.shape[1]
    slots = tile_pix // 2
    sent = compact(frames, frame_valid, valid_count, block_map)
    tile_frames = lax.all_to_all(sent, "tm", split_axis=0, concat_axis=0, tiled=True)
    if frame_dev // RADIX % 16 != 0:
        tile_frames = tile_frames.reshape(devices, RADIX, frame_dev // RADIX, slots)
        tile_frames = tile_frames.transpose(1, 0, 2, 3).reshape(RADIX, frames_len // RADIX, slots)
    place, own_map, own_count = neighbour_places(valid_count, block_map, position)
    own, left, right = transform(place, tile_frames, slots, frames_len)
    from_right = lax.ppermute(left, "tm", [(i, i - 1) for i in range(1, devices)])
    from_left = lax.ppermute(right, "tm", [(i, i + 1) for i in range(devices - 1)])
    tile_width = tile_pix // ROWS
    result = cross(place, offsets, own_map, own_count, own, from_right, from_left, tile_width)
    bins = frames_len // 2
    result = result.reshape(tile_width, offsets.shape[0], bins // LANES, 2, LANES)
    return result.transpose(0, 1, 3, 2, 4).reshape(tile_width, offsets.shape[0], 2, bins)


def solution(mesh):
    return jax.shard_map(
        per_device,
        mesh=mesh,
        in_specs=(P("tm", "groups"), P(("groups", "tm")), P("groups"), P("groups", None), P()),
        out_specs=P(("groups", "tm"), None, None, None),
        check_vma=False,
    )
```

```python
import functools
import math

import jax
import jax.numpy as jnp
import numpy as np
from jax import lax
from jax.experimental import pallas as pl
from jax.experimental.pallas import tpu as pltpu
from jax.sharding import PartitionSpec as P

ROWS = 16
REACH = 4
RADIX = 16
LANES = 128
INFO = 10


def dft_tables(frames_len):
    inner = frames_len // RADIX
    steps = np.arange(inner)
    angles = 2.0 * np.pi * (np.outer(steps, steps) % inner) / inner
    table = np.concatenate([np.cos(angles), -np.sin(angles)], axis=1) / math.sqrt(frames_len)
    turns = 2.0 * np.pi * np.outer(np.arange(RADIX), steps) / frames_len
    twiddle = np.stack([np.cos(turns), -np.sin(turns)], axis=1)
    twiddle = np.broadcast_to(twiddle[:, :, None, :], (RADIX, 2, 8, inner))
    return jnp.asarray(table, jnp.bfloat16), jnp.asarray(twiddle, jnp.float32)


def compact_kernel(count_ref, valid_ref, map_ref, frames_ref, out_ref, keep, rows):
    step = pl.program_id(0)
    batch, frame_dev, slots = out_ref.shape
    tile_pix = frames_ref.shape[1] // batch
    per_phase = frame_dev // RADIX
    pitch = RADIX + 1

    @pl.when(step == 0)
    def _():
        row = lax.broadcasted_iota(jnp.int32, (frame_dev, frame_dev), 0)
        col = lax.broadcasted_iota(jnp.int32, (frame_dev, frame_dev), 1)
        source = row % per_phase * RADIX + row // per_phase
        usable = jnp.broadcast_to(valid_ref[...], (frame_dev, frame_dev))
        order = jnp.where(col == source, usable, 0).astype(jnp.float32).astype(jnp.bfloat16)
        ones = jnp.ones((frame_dev, slots), jnp.bfloat16)
        keep[...] = jnp.dot(order, ones, preferred_element_type=jnp.float32)

    pixel = lax.broadcasted_iota(jnp.int32, (tile_pix, slots), 0)
    slot = lax.broadcasted_iota(jnp.int32, (1, slots), 1)
    tiles = lax.broadcasted_iota(jnp.int32, (map_ref.shape[0], slots), 0)
    for which in range(batch):
        tile = step * batch + which
        row = jnp.sum(jnp.where(tiles == tile, map_ref[:, :slots], 0), axis=0, keepdims=True)
        held = jnp.where(slot < count_ref[tile], row, -1)
        hot = jnp.where(jnp.broadcast_to(held, (tile_pix, slots)) == pixel, 1.0, 0.0).astype(jnp.bfloat16)
        block = frames_ref[:, which * tile_pix : (which + 1) * tile_pix]
        picked = jnp.dot(block, hot, preferred_element_type=jnp.float32)
        for part in range(per_phase):
            rows[which, pl.ds(part * pitch, RADIX), :] = picked[part * RADIX : (part + 1) * RADIX, :]
        for phase in range(RADIX):
            span = pl.ds(phase * per_phase, per_phase)
            taken = rows[which, pl.ds(phase, per_phase, stride=pitch), :] * keep[span, :]
            out_ref[which, span, :] = taken.astype(jnp.bfloat16)


def compact(frames, frame_valid, valid_count, block_map):
    frame_dev, pixel_count = frames.shape
    tile_count, tile_pix = block_map.shape
    slots = tile_pix // 2
    batch = 4
    return pl.pallas_call(
        compact_kernel,
        name="compact",
        grid=(tile_count // batch,),
        out_shape=jax.ShapeDtypeStruct((tile_count, frame_dev, slots), jnp.bfloat16),
        in_specs=[
            pl.BlockSpec(memory_space=pltpu.SMEM),
            pl.BlockSpec((1, frame_dev), lambda i: (0, 0)),
            pl.BlockSpec((tile_count, tile_pix), lambda i: (0, 0)),
            pl.BlockSpec((frame_dev, batch * tile_pix), lambda i: (0, i)),
        ],
        out_specs=pl.BlockSpec((batch, frame_dev, slots), lambda i: (i, 0, 0)),
        scratch_shapes=[
            pltpu.VMEM((frame_dev, slots), jnp.float32),
            pltpu.VMEM((batch, frame_dev // RADIX * (RADIX + 1) + 7, slots), jnp.float32),
        ],
    )(valid_count, frame_valid.reshape(1, frame_dev), block_map, frames)


def rotate(real, imag, cos, sin):
    return real * cos - imag * sin, real * sin + imag * cos


def four_point(values):
    (r0, i0), (r1, i1), (r2, i2), (r3, i3) = values
    er, ei, fr, fi = r0 + r2, i0 + i2, r0 - r2, i0 - i2
    gr, gi, hr, hi = r1 + r3, i1 + i3, r1 - r3, i1 - i3
    return [(er + gr, ei + gi), (fr + hi, fi - hr), (er - gr, ei - gi), (fr - hi, fi + hr)]


def sixteen_point_low(values):
    inner = [four_point([values[4 * n + m] for n in range(4)]) for m in range(4)]
    low = [None] * 8
    for k in range(4):
        parts = []
        for m in range(4):
            real, imag = inner[m][k]
            turn = m * k % 16
            if turn == 0:
                parts.append((real, imag))
            elif turn == 4:
                parts.append((imag, -real))
            else:
                angle = -2.0 * math.pi * turn / 16
                parts.append(rotate(real, imag, math.cos(angle), math.sin(angle)))
        (r0, i0), (r1, i1), (r2, i2), (r3, i3) = parts
        low[k] = ((r0 + r2) + (r1 + r3), (i0 + i2) + (i1 + i3))
        low[k + 4] = ((r0 - r2) + (i1 - i3), (i0 - i2) - (r1 - r3))
    return low


def transform_kernel(info_ref, frames_ref, table_ref, twiddle_ref, own_ref, near_ref, far_ref, phases, spread):
    slots = own_ref.shape[0]
    rows = own_ref.shape[1]
    pitch = rows + 1
    half = rows // 2
    inner = table_ref.shape[0]
    places = info_ref.shape[0] - slots - INFO
    width = places // (ROWS + 2 * REACH)
    for phase in range(RADIX):
        if len(frames_ref.shape) == 3:
            per_phase = frames_ref.shape[1] // RADIX
            block = frames_ref[:, phase * per_phase : (phase + 1) * per_phase, :].reshape(inner, slots)
        else:
            block = frames_ref[phase].reshape(inner, slots)
        phases[phase] = lax.dot_general(
            block, table_ref[...], (((0,), (0,)), ((), ())), preferred_element_type=jnp.float32
        )
    chunks = inner // LANES

    def one_group(group, carry):
        first = pl.multiple_of(group * 8, 8)
        for chunk in range(chunks):
            lanes = pl.ds(chunk * LANES, LANES)
            values = []
            for phase in range(RADIX):
                real = phases[phase, pl.ds(first, 8), lanes]
                imag = phases[phase, pl.ds(first, 8), pl.ds(inner + chunk * LANES, LANES)]
                if phase > 0:
                    real, imag = rotate(real, imag, twiddle_ref[phase, 0, :, lanes], twiddle_ref[phase, 1, :, lanes])
                values.append((real, imag))
            for high, (real, imag) in enumerate(sixteen_point_low(values)):
                at = first * pitch + high * chunks + chunk
                spread[pl.ds(at, 8, stride=pitch), :] = real
                spread[pl.ds(at + half, 8, stride=pitch), :] = imag
        return carry

    lax.fori_loop(0, slots // 8, one_group, 0)

    def one_slot(slot, carry):
        own_ref[slot] = spread[pl.ds(slot * pitch, rows), :].astype(jnp.bfloat16)
        return carry

    lax.fori_loop(0, slots, one_slot, 0, unroll=8)
    odd = info_ref[places]
    near_side = jnp.where(odd == 1, 0, width - 3 * REACH)
    far_side = jnp.where(odd == 1, width - 3 * REACH, 0)

    def one_edge(row, carry):
        for column in range(REACH):
            base = (row + REACH) * width + REACH + column
            spot = row * REACH + column
            near_ref[spot] = own_ref[jnp.minimum(info_ref[base + near_side], slots - 1)]
            far_ref[spot] = own_ref[jnp.minimum(info_ref[base + far_side], slots - 1)]
        return carry

    lax.fori_loop(0, ROWS, one_edge, 0, unroll=2)


def transform(info, tile_frames, slots, frames_len):
    table, twiddle = dft_tables(frames_len)
    inner = frames_len // RADIX
    rows = frames_len // LANES
    edge = ROWS * REACH
    whole = pl.BlockSpec(memory_space=pltpu.VMEM)
    return pl.pallas_call(
        transform_kernel,
        name="transform",
        out_shape=(
            jax.ShapeDtypeStruct((slots, rows, LANES), jnp.bfloat16),
            jax.ShapeDtypeStruct((edge, rows, LANES), jnp.bfloat16),
            jax.ShapeDtypeStruct((edge, rows, LANES), jnp.bfloat16),
        ),
        in_specs=[pl.BlockSpec(memory_space=pltpu.SMEM), whole, whole, whole],
        out_specs=(whole, whole, whole),
        scratch_shapes=[
            pltpu.VMEM((RADIX, slots, 2 * inner), jnp.float32),
            pltpu.VMEM((slots * (rows + 1) + 7, LANES), jnp.float32),
        ],
        compiler_params=pltpu.CompilerParams(vmem_limit_bytes=24 * 2**20),
    )(info, tile_frames, table, twiddle)


def inside_kernel(info_ref, own_hbm, out_ref, scale_ref, list_ref, held, *rest):
    totals, (pairs, sem) = rest[:-2], rest[-2:]
    slots, rows, _ = own_hbm.shape
    half = rows // 2
    edge = ROWS * REACH
    places = info_ref.shape[0] - slots - INFO
    width = places // (ROWS + 2 * REACH)
    tile_width = width - 2 * REACH
    empty = slots + 2 * edge
    offsets = len(totals)
    copy = pltpu.make_async_copy(own_hbm, held.at[pl.ds(0, slots)], sem)
    copy.start()
    held[slots] = jnp.zeros((rows, LANES), jnp.bfloat16)
    for total in totals:
        total[...] = jnp.zeros(total.shape, jnp.float32)

    def clear(spot, carry):
        pairs[spot] = 0
        return carry

    lax.fori_loop(0, pairs.shape[0], clear, 0, unroll=8)
    shifts = [info_ref[places + 2 + 2 * j] * width + info_ref[places + 3 + 2 * j] for j in range(offsets)]
    copy.wait()

    def one_slot(slot, listed):
        pixel = info_ref[places + INFO + slot]
        row = pixel // tile_width
        column = pixel % tile_width
        base = (row + REACH) * width + REACH + column
        own_real = held[slot, :half].astype(jnp.float32)
        own_imag = held[slot, half:].astype(jnp.float32)
        for j, total in enumerate(totals):
            other = info_ref[base + shifts[j]]
            at = column * offsets + j
            pairs[at] = pairs[at] + jnp.where(other < empty, 1, 0)
            list_ref[1 + listed] = (at * empty + other) * slots + slot
            listed = listed + jnp.where((other < empty) & (other >= slots), 1, 0)
            within = jnp.minimum(other, slots)
            real = held[within, :half].astype(jnp.float32)
            imag = held[within, half:].astype(jnp.float32)
            total[column, :half] += own_real * real + own_imag * imag
            total[column, half:] += own_imag * real - own_real * imag
        return listed

    list_ref[0] = lax.fori_loop(0, info_ref[places + 1], one_slot, 0)

    def finish(column, carry):
        for j, total in enumerate(totals):
            at = column * offsets + j
            seen = jnp.full((1, LANES), pairs[at], jnp.int32).astype(jnp.float32)
            scaling = 1.0 / jnp.maximum(seen, 1.0)
            scale_ref[pl.ds(at, 1), :] = scaling
            out_ref[at, pl.ds(0, half, stride=2), :] = total[column, :half] * scaling
            out_ref[at, pl.ds(1, half, stride=2), :] = total[column, half:] * scaling
        return carry

    lax.fori_loop(0, tile_width, finish, 0)


def inside(info, own, tile_width, offsets):
    slots, rows, _ = own.shape
    spots = tile_width * offsets
    small = pl.BlockSpec(memory_space=pltpu.SMEM)
    whole = pl.BlockSpec(memory_space=pltpu.VMEM)
    return pl.pallas_call(
        inside_kernel,
        name="inside",
        out_shape=(
            jax.ShapeDtypeStruct((spots, rows, LANES), jnp.float32),
            jax.ShapeDtypeStruct((spots, LANES), jnp.float32),
            jax.ShapeDtypeStruct((slots * offsets + 2,), jnp.int32),
        ),
        in_specs=[small, pl.BlockSpec(memory_space=pl.ANY)],
        out_specs=(whole, whole, small),
        scratch_shapes=[pltpu.VMEM((slots + 1, rows, LANES), jnp.bfloat16)]
        + [pltpu.VMEM((tile_width, rows, LANES), jnp.float32)] * offsets
        + [pltpu.SMEM((spots,), jnp.int32), pltpu.SemaphoreType.DMA],
        compiler_params=pltpu.CompilerParams(vmem_limit_bytes=16 * 2**20),
        cost_estimate=pl.CostEstimate(flops=60_000_000, bytes_accessed=4_000_000, transcendentals=0),
    )(info, own)


def across_kernel(list_ref, scale_ref, own_ref, near_ref, far_ref, part_ref, out_ref):
    slots, rows, _ = own_ref.shape
    edge = near_ref.shape[0]
    half = rows // 2
    empty = slots + 2 * edge
    out_ref[...] = part_ref[...]

    def one_pair(pair, carry):
        code = list_ref[1 + pair]
        slot = code % slots
        other = code // slots % empty - slots
        at = code // slots // empty
        scaling = scale_ref[pl.ds(at, 1), :]
        own_real = own_ref[slot, :half].astype(jnp.float32) * scaling
        own_imag = own_ref[slot, half:].astype(jnp.float32) * scaling
        from_near = other < edge
        close = jnp.minimum(other, edge - 1)
        distant = jnp.maximum(other - edge, 0)
        both = jnp.where(from_near, near_ref[close], far_ref[distant]).astype(jnp.float32)
        real, imag = both[:half], both[half:]
        out_ref[at, pl.ds(0, half, stride=2), :] += own_real * real + own_imag * imag
        out_ref[at, pl.ds(1, half, stride=2), :] += own_imag * real - own_real * imag
        return carry

    lax.fori_loop(0, list_ref[0], one_pair, 0)


def across(listed, scale, own, near, far, part):
    small = pl.BlockSpec(memory_space=pltpu.SMEM)
    whole = pl.BlockSpec(memory_space=pltpu.VMEM)
    return pl.pallas_call(
        across_kernel,
        name="across",
        out_shape=jax.ShapeDtypeStruct(part.shape, part.dtype),
        in_specs=[small, whole, whole, whole, whole, whole],
        out_specs=whole,
        compiler_params=pltpu.CompilerParams(vmem_limit_bytes=16 * 2**20),
    )(listed, scale, own, near, far, part)


def describe(valid_count, block_map, offsets, position):
    tile_pix = block_map.shape[1]
    slots = tile_pix // 2
    tile_width = tile_pix // ROWS
    edge = ROWS * REACH
    empty = slots + 2 * edge
    padded_count = jnp.pad(valid_count, ((1, 1),))
    padded_map = jnp.pad(block_map, ((1, 1), (0, 0)))
    counts = lax.dynamic_slice_in_dim(padded_count, position, 3, 0)
    maps = lax.dynamic_slice_in_dim(padded_map, position, 3, 0)[:, :slots]
    slot_idx = jnp.arange(slots, dtype=jnp.int32)
    pixel_idx = jnp.arange(tile_pix, dtype=jnp.int32)
    match = (maps[:, :, None] == pixel_idx[None, None, :]) & (slot_idx[None, :, None] < counts[:, None, None])
    found = jnp.max(jnp.where(match, slot_idx[None, :, None], -1), axis=1)
    grid = found.reshape(3, ROWS, tile_width)
    spot = (jnp.arange(ROWS, dtype=jnp.int32) * REACH)[:, None] + jnp.arange(REACH, dtype=jnp.int32)[None, :]
    odd = position % 2
    own = jnp.where(grid[1] >= 0, grid[1], empty)
    right = jnp.where(grid[2][:, :REACH] >= 0, slots + odd * edge + spot, empty)
    left = jnp.where(grid[0][:, tile_width - REACH :] >= 0, slots + (1 - odd) * edge + spot, empty)
    place = jnp.concatenate([left, own, right], axis=1)
    place = jnp.pad(place, ((REACH, REACH), (0, 0)), constant_values=empty)
    head = jnp.stack([odd.astype(jnp.int32), counts[1]])
    return jnp.concatenate([place.reshape(-1), head, offsets.reshape(-1), maps[1]])


def per_device(frames, frame_valid, valid_count, block_map, offsets):
    devices = lax.axis_size("tm")
    position = lax.axis_index("tm")
    frame_dev = frames.shape[0]
    frames_len = frame_dev * devices
    tile_pix = block_map.shape[1]
    slots = tile_pix // 2
    tile_width = tile_pix // ROWS
    sent = compact(frames, frame_valid, valid_count, block_map)
    tile_frames = lax.all_to_all(sent, "tm", split_axis=0, concat_axis=0, tiled=True)
    if frame_dev // RADIX % 16 != 0:
        tile_frames = tile_frames.reshape(devices, RADIX, frame_dev // RADIX, slots)
        tile_frames = tile_frames.transpose(1, 0, 2, 3).reshape(RADIX, frames_len // RADIX, slots)
    info = describe(valid_count, block_map, offsets, position)
    own, near, far = transform(info, tile_frames, slots, frames_len)
    far_pairs = [(i, i + 1) for i in range(1, devices - 1, 2)] + [(i + 1, i) for i in range(1, devices - 1, 2)]
    near_pairs = [(i, i + 1) for i in range(0, devices - 1, 2)] + [(i + 1, i) for i in range(0, devices - 1, 2)]
    far = lax.ppermute(far, "tm", far_pairs)
    near = lax.ppermute(near, "tm", near_pairs)
    part, scale, listed = inside(info, own, tile_width, offsets.shape[0])
    result = across(listed, scale, own, near, far, part)
    bins = frames_len // 2
    result = result.reshape(tile_width, offsets.shape[0], bins // LANES, 2, LANES)
    return result.transpose(0, 1, 3, 2, 4).reshape(tile_width, offsets.shape[0], 2, bins)


def solution(mesh):
    return jax.shard_map(
        per_device,
        mesh=mesh,
        in_specs=(P("tm", "groups"), P(("groups", "tm")), P("groups"), P("groups", None), P()),
        out_specs=P(("groups", "tm"), None, None, None),
        check_vma=False,
    )
```

```python
import functools
import math

import jax
import jax.numpy as jnp
import numpy as np
from jax import lax
from jax.experimental import pallas as pl
from jax.experimental.pallas import tpu as pltpu
from jax.sharding import PartitionSpec as P

ROWS = 16
REACH = 4
RADIX = 16
LANES = 128
INFO = 10


def dft_tables(frames_len):
    inner = frames_len // RADIX
    steps = np.arange(inner)
    angles = 2.0 * np.pi * (np.outer(steps, steps) % inner) / inner
    table = np.concatenate([np.cos(angles), -np.sin(angles)], axis=1) / math.sqrt(frames_len)
    turns = 2.0 * np.pi * np.outer(np.arange(RADIX), steps) / frames_len
    twiddle = np.stack([np.cos(turns), -np.sin(turns)], axis=1)
    twiddle = np.broadcast_to(twiddle[:, :, None, :], (RADIX, 2, 8, inner))
    return jnp.asarray(table, jnp.bfloat16), jnp.asarray(twiddle, jnp.float32)


def compact_kernel(count_hbm, valid_hbm, map_hbm, frames_hbm, out_hbm, frames, out_ref, keep, rows, count_ref, valid_ref, map_ref, sems, out_sems, small_sems):
    tile_count, frame_dev, slots = out_ref.shape
    tile_pix = map_ref.shape[1]
    batch = frames.shape[2] // tile_pix
    per_phase = frame_dev // RADIX
    pitch = RADIX + 1
    copies = []
    for step in range(frames.shape[0]):
        span = pl.ds(step * batch * tile_pix, batch * tile_pix)
        copies.append(pltpu.make_async_copy(frames_hbm.at[:, span], frames.at[step], sems.at[step]))
        copies[-1].start()
    smalls = [
        pltpu.make_async_copy(valid_hbm, valid_ref, small_sems.at[0]),
        pltpu.make_async_copy(map_hbm, map_ref, small_sems.at[1]),
        pltpu.make_async_copy(count_hbm, count_ref, small_sems.at[2]),
    ]
    for small in smalls:
        small.start()
    for small in smalls:
        small.wait()
    row = lax.broadcasted_iota(jnp.int32, (frame_dev, frame_dev), 0)
    col = lax.broadcasted_iota(jnp.int32, (frame_dev, frame_dev), 1)
    source = row % per_phase * RADIX + row // per_phase
    usable = jnp.broadcast_to(valid_ref[...], (frame_dev, frame_dev))
    order = jnp.where(col == source, usable, 0).astype(jnp.float32).astype(jnp.bfloat16)
    ones = jnp.ones((frame_dev, slots), jnp.bfloat16)
    keep[...] = jnp.dot(order, ones, preferred_element_type=jnp.float32)
    pixel = lax.broadcasted_iota(jnp.int32, (tile_pix, slots), 0)
    slot = lax.broadcasted_iota(jnp.int32, (1, slots), 1)

    def one_tile(step, which):
        tile = step * batch + which
        held = jnp.where(slot < count_ref[tile], map_ref[tile : tile + 1, :slots], -1)
        hot = jnp.where(jnp.broadcast_to(held, (tile_pix, slots)) == pixel, 1.0, 0.0).astype(jnp.bfloat16)
        block = frames[step, :, which * tile_pix : (which + 1) * tile_pix]
        picked = jnp.dot(block, hot, preferred_element_type=jnp.float32)
        for part in range(per_phase):
            rows[which, pl.ds(part * pitch, RADIX), :] = picked[part * RADIX : (part + 1) * RADIX, :]
        for phase in range(RADIX):
            span = pl.ds(phase * per_phase, per_phase)
            taken = rows[which, pl.ds(phase, per_phase, stride=pitch), :] * keep[span, :]
            out_ref[tile, span, :] = taken.astype(jnp.bfloat16)

    for step, copy in enumerate(copies):
        copy.wait()
        for which in range(batch):
            one_tile(step, which)
        span = pl.ds(step * batch, batch)
        copies[step] = pltpu.make_async_copy(out_ref.at[span], out_hbm.at[span], out_sems.at[step])
        copies[step].start()
    for copy in copies:
        copy.wait()


def compact(frames, frame_valid, valid_count, block_map):
    frame_dev, pixel_count = frames.shape
    tile_count, tile_pix = block_map.shape
    slots = tile_pix // 2
    batch = 4
    steps = tile_count // batch
    place = pl.BlockSpec(memory_space=pl.ANY)
    return pl.pallas_call(
        compact_kernel,
        name="compact",
        out_shape=jax.ShapeDtypeStruct((tile_count, frame_dev, slots), jnp.bfloat16),
        in_specs=[place] * 4,
        out_specs=place,
        scratch_shapes=[
            pltpu.VMEM((steps, frame_dev, batch * tile_pix), jnp.bfloat16),
            pltpu.VMEM((tile_count, frame_dev, slots), jnp.bfloat16),
            pltpu.VMEM((frame_dev, slots), jnp.float32),
            pltpu.VMEM((batch, frame_dev // RADIX * (RADIX + 1) + 7, slots), jnp.float32),
            pltpu.SMEM((tile_count,), jnp.int32),
            pltpu.VMEM((1, frame_dev), jnp.int32),
            pltpu.VMEM((tile_count, tile_pix), jnp.int32),
            pltpu.SemaphoreType.DMA((steps,)),
            pltpu.SemaphoreType.DMA((steps,)),
            pltpu.SemaphoreType.DMA((3,)),
        ],
        compiler_params=pltpu.CompilerParams(vmem_limit_bytes=62 * 2**20),
    )(valid_count, frame_valid.reshape(1, frame_dev), block_map, frames)


def rotate(real, imag, cos, sin):
    return real * cos - imag * sin, real * sin + imag * cos


def four_point(values):
    (r0, i0), (r1, i1), (r2, i2), (r3, i3) = values
    er, ei, fr, fi = r0 + r2, i0 + i2, r0 - r2, i0 - i2
    gr, gi, hr, hi = r1 + r3, i1 + i3, r1 - r3, i1 - i3
    return [(er + gr, ei + gi), (fr + hi, fi - hr), (er - gr, ei - gi), (fr - hi, fi + hr)]


def sixteen_point_low(values):
    inner = [four_point([values[4 * n + m] for n in range(4)]) for m in range(4)]
    low = [None] * 8
    for k in range(4):
        parts = []
        for m in range(4):
            real, imag = inner[m][k]
            turn = m * k % 16
            if turn == 0:
                parts.append((real, imag))
            elif turn == 4:
                parts.append((imag, -real))
            else:
                angle = -2.0 * math.pi * turn / 16
                parts.append(rotate(real, imag, math.cos(angle), math.sin(angle)))
        (r0, i0), (r1, i1), (r2, i2), (r3, i3) = parts
        low[k] = ((r0 + r2) + (r1 + r3), (i0 + i2) + (i1 + i3))
        low[k + 4] = ((r0 - r2) + (i1 - i3), (i0 - i2) - (r1 - r3))
    return low


def transform_kernel(info_ref, frames_ref, table_ref, twiddle_ref, own_ref, *rest):
    (edges, (phases, spread)) = rest[:-2], rest[-2:]
    slots = own_ref.shape[0]
    rows = own_ref.shape[1]
    pitch = rows + 1
    half = rows // 2
    inner = table_ref.shape[0]
    half_edge = ROWS * REACH // 2
    lists = info_ref.shape[0] - 4 * half_edge
    for phase in range(RADIX):
        if len(frames_ref.shape) == 3:
            per_phase = frames_ref.shape[1] // RADIX
            block = frames_ref[:, phase * per_phase : (phase + 1) * per_phase, :].reshape(inner, slots)
        else:
            block = frames_ref[phase].reshape(inner, slots)
        phases[phase] = lax.dot_general(
            block, table_ref[...], (((0,), (0,)), ((), ())), preferred_element_type=jnp.float32
        )
    chunks = inner // LANES

    def one_group(group, carry):
        first = pl.multiple_of(group * 8, 8)
        for chunk in range(chunks):
            lanes = pl.ds(chunk * LANES, LANES)
            values = []
            for phase in range(RADIX):
                real = phases[phase, pl.ds(first, 8), lanes]
                imag = phases[phase, pl.ds(first, 8), pl.ds(inner + chunk * LANES, LANES)]
                if phase > 0:
                    real, imag = rotate(real, imag, twiddle_ref[phase, 0, :, lanes], twiddle_ref[phase, 1, :, lanes])
                values.append((real, imag))
            for high, (real, imag) in enumerate(sixteen_point_low(values)):
                at = first * pitch + high * chunks + chunk
                spread[pl.ds(at, 8, stride=pitch), :] = real
                spread[pl.ds(at + half, 8, stride=pitch), :] = imag
        return carry

    lax.fori_loop(0, slots // 8, one_group, 0)

    def one_slot(slot, carry):
        own_ref[slot] = spread[pl.ds(slot * pitch, rows), :].astype(jnp.bfloat16)
        return carry

    lax.fori_loop(0, slots, one_slot, 0, unroll=8)

    def one_edge(spot, carry):
        for part, edge_ref in enumerate(edges):
            edge_ref[spot] = own_ref[info_ref[lists + part * half_edge + spot]]
        return carry

    lax.fori_loop(0, half_edge, one_edge, 0, unroll=4)


def transform(info, tile_frames, slots, frames_len):
    table, twiddle = dft_tables(frames_len)
    inner = frames_len // RADIX
    rows = frames_len // LANES
    edge = ROWS * REACH
    whole = pl.BlockSpec(memory_space=pltpu.VMEM)
    return pl.pallas_call(
        transform_kernel,
        name="transform",
        out_shape=(
            jax.ShapeDtypeStruct((slots, rows, LANES), jnp.bfloat16),
            *[jax.ShapeDtypeStruct((edge // 2, rows, LANES), jnp.bfloat16)] * 4,
        ),
        in_specs=[pl.BlockSpec(memory_space=pltpu.SMEM), whole, whole, whole],
        out_specs=(whole,) * 5,
        scratch_shapes=[
            pltpu.VMEM((RADIX, slots, 2 * inner), jnp.float32),
            pltpu.VMEM((slots * (rows + 1) + 7, LANES), jnp.float32),
        ],
        compiler_params=pltpu.CompilerParams(vmem_limit_bytes=24 * 2**20),
    )(info, tile_frames, table, twiddle)


def inside_kernel(info_ref, own_hbm, out_ref, scale_ref, list_ref, held, *rest):
    totals, (pairs, sem) = rest[:-2], rest[-2:]
    slots, rows, _ = own_hbm.shape
    half = rows // 2
    edge = ROWS * REACH
    places = info_ref.shape[0] - slots - INFO - 2 * edge
    width = places // (ROWS + 2 * REACH)
    tile_width = width - 2 * REACH
    empty = slots + 2 * edge
    offsets = len(totals)
    copy = pltpu.make_async_copy(own_hbm, held.at[pl.ds(0, slots)], sem)
    copy.start()
    held[slots] = jnp.zeros((rows, LANES), jnp.bfloat16)
    for total in totals:
        total[...] = jnp.zeros(total.shape, jnp.float32)

    def clear(spot, carry):
        pairs[spot] = 0
        return carry

    lax.fori_loop(0, pairs.shape[0], clear, 0, unroll=8)
    shifts = [info_ref[places + 2 + 2 * j] * width + info_ref[places + 3 + 2 * j] for j in range(offsets)]
    copy.wait()

    def one_slot(slot, listed):
        pixel = info_ref[places + INFO + slot]
        row = pixel // tile_width
        column = pixel % tile_width
        base = (row + REACH) * width + REACH + column
        own_real = held[slot, :half].astype(jnp.float32)
        own_imag = held[slot, half:].astype(jnp.float32)
        for j, total in enumerate(totals):
            other = info_ref[base + shifts[j]]
            at = column * offsets + j
            pairs[at] = pairs[at] + jnp.where(other < empty, 1, 0)
            list_ref[1 + listed] = (at * empty + other) * slots + slot
            listed = listed + jnp.where((other < empty) & (other >= slots), 1, 0)
            within = jnp.minimum(other, slots)
            real = held[within, :half].astype(jnp.float32)
            imag = held[within, half:].astype(jnp.float32)
            total[column, :half] += own_real * real + own_imag * imag
            total[column, half:] += own_imag * real - own_real * imag
        return listed

    list_ref[0] = lax.fori_loop(0, info_ref[places + 1], one_slot, 0)

    def finish(column, carry):
        for j, total in enumerate(totals):
            at = column * offsets + j
            seen = jnp.full((1, LANES), pairs[at], jnp.int32).astype(jnp.float32)
            scaling = 1.0 / jnp.maximum(seen, 1.0)
            scale_ref[pl.ds(at, 1), :] = scaling
            out_ref[at, pl.ds(0, half, stride=2), :] = total[column, :half] * scaling
            out_ref[at, pl.ds(1, half, stride=2), :] = total[column, half:] * scaling
        return carry

    lax.fori_loop(0, tile_width, finish, 0)


def inside(info, own, tile_width, offsets):
    slots, rows, _ = own.shape
    spots = tile_width * offsets
    small = pl.BlockSpec(memory_space=pltpu.SMEM)
    whole = pl.BlockSpec(memory_space=pltpu.VMEM)
    return pl.pallas_call(
        inside_kernel,
        name="inside",
        out_shape=(
            jax.ShapeDtypeStruct((spots, rows, LANES), jnp.float32),
            jax.ShapeDtypeStruct((spots, LANES), jnp.float32),
            jax.ShapeDtypeStruct((slots * offsets + 2,), jnp.int32),
        ),
        in_specs=[small, pl.BlockSpec(memory_space=pl.ANY)],
        out_specs=(whole, whole, small),
        scratch_shapes=[pltpu.VMEM((slots + 1, rows, LANES), jnp.bfloat16)]
        + [pltpu.VMEM((tile_width, rows, LANES), jnp.float32)] * offsets
        + [pltpu.SMEM((spots,), jnp.int32), pltpu.SemaphoreType.DMA],
        compiler_params=pltpu.CompilerParams(vmem_limit_bytes=16 * 2**20),
        cost_estimate=pl.CostEstimate(flops=60_000_000, bytes_accessed=4_000_000, transcendentals=0),
    )(info, own)


def across_kernel(list_ref, scale_ref, own_ref, near_ref, far_ref, part_ref, out_ref):
    slots, rows, _ = own_ref.shape
    edge = ROWS * REACH
    sent = near_ref.shape[0]
    half = rows // 2
    empty = slots + 2 * edge
    out_ref[...] = part_ref[...]

    def one_pair(pair, carry):
        code = list_ref[1 + pair]
        slot = code % slots
        other = code // slots % empty - slots
        at = code // slots // empty
        scaling = scale_ref[pl.ds(at, 1), :]
        own_real = own_ref[slot, :half].astype(jnp.float32) * scaling
        own_imag = own_ref[slot, half:].astype(jnp.float32) * scaling
        from_near = other < edge
        close = jnp.minimum(other, sent - 1)
        distant = jnp.maximum(other - edge, 0)
        both = jnp.where(from_near, near_ref[close], far_ref[distant]).astype(jnp.float32)
        real, imag = both[:half], both[half:]
        out_ref[at, pl.ds(0, half, stride=2), :] += own_real * real + own_imag * imag
        out_ref[at, pl.ds(1, half, stride=2), :] += own_imag * real - own_real * imag
        return carry

    lax.fori_loop(0, list_ref[0], one_pair, 0)


def across(listed, scale, own, near, far, part):
    small = pl.BlockSpec(memory_space=pltpu.SMEM)
    whole = pl.BlockSpec(memory_space=pltpu.VMEM)
    return pl.pallas_call(
        across_kernel,
        name="across",
        out_shape=jax.ShapeDtypeStruct(part.shape, part.dtype),
        in_specs=[small, whole, whole, whole, whole, whole],
        out_specs=whole,
        compiler_params=pltpu.CompilerParams(vmem_limit_bytes=16 * 2**20),
    )(listed, scale, own, near, far, part)


def describe(valid_count, block_map, offsets, position):
    tile_count, tile_pix = block_map.shape
    slots = tile_pix // 2
    tile_width = tile_pix // ROWS
    edge = ROWS * REACH
    empty = slots + 2 * edge
    columns = tile_count * tile_width
    slot_idx = jnp.arange(slots, dtype=jnp.int32)
    pixel_idx = jnp.arange(tile_pix, dtype=jnp.int32)
    held = jnp.where(slot_idx[None, :] < valid_count[:, None], block_map[:, :slots], -1)
    found = jnp.max(jnp.where(held[:, :, None] == pixel_idx, slot_idx[None, :, None], -1), axis=1)
    cells = found.reshape(tile_count, ROWS, tile_width)
    valid = (cells >= 0).astype(jnp.int32)
    grid = valid.transpose(1, 0, 2).reshape(ROWS, columns)
    padded = jnp.pad(grid, ((REACH, REACH), (REACH, REACH)))
    local = jnp.arange(columns, dtype=jnp.int32)[None, :] % tile_width
    for_left = jnp.zeros_like(grid)
    for_right = jnp.zeros_like(grid)
    for j in range(offsets.shape[0]):
        partner = lax.dynamic_slice(padded, (REACH - offsets[j, 0], REACH - offsets[j, 1]), (ROWS, columns))
        for_left = jnp.where(local < offsets[j, 1], jnp.maximum(for_left, partner), for_left)
        for_right = jnp.where(local - offsets[j, 1] >= tile_width, jnp.maximum(for_right, partner), for_right)

    def numbered(needed, first):
        needed = (needed * grid).reshape(ROWS, tile_count, tile_width)[:, :, first : first + REACH]
        needed = needed.transpose(1, 0, 2).reshape(tile_count, edge)
        before = (jnp.arange(edge)[:, None] < jnp.arange(edge)[None, :]).astype(jnp.bfloat16)
        rank = jnp.dot(needed.astype(jnp.bfloat16), before, preferred_element_type=jnp.float32).astype(jnp.int32)
        at = cells[:, :, first : first + REACH].reshape(tile_count, edge)
        return jnp.where(needed > 0, rank, edge), at

    left_rank, left_slot = numbered(for_left, 0)
    right_rank, right_slot = numbered(for_right, tile_width - REACH)
    most = jnp.maximum(jnp.max(jnp.where(left_rank < edge, left_rank, -1)), jnp.max(jnp.where(right_rank < edge, right_rank, -1)))
    few = most < edge // 2

    def own_list(ranks, at):
        own_rank = lax.dynamic_index_in_dim(ranks, position, 0, keepdims=False)
        own_at = lax.dynamic_index_in_dim(at, position, 0, keepdims=False)
        return jnp.max(jnp.where(own_rank[:, None] == jnp.arange(edge)[None, :], own_at[:, None], 0), axis=0)

    odd = position % 2
    left_list = own_list(left_rank, left_slot)
    right_list = own_list(right_rank, right_slot)
    near_list = jnp.where(odd == 1, left_list, right_list)
    far_list = jnp.where(odd == 1, right_list, left_list)
    above = lax.dynamic_index_in_dim(jnp.pad(left_rank, ((0, 1), (0, 0)), constant_values=edge), position + 1, 0, keepdims=False)
    below = lax.dynamic_index_in_dim(jnp.pad(right_rank, ((1, 0), (0, 0)), constant_values=edge), position, 0, keepdims=False)
    right = jnp.where(above < edge, slots + odd * edge + above, empty).reshape(ROWS, REACH)
    left = jnp.where(below < edge, slots + (1 - odd) * edge + below, empty).reshape(ROWS, REACH)
    own = lax.dynamic_index_in_dim(cells, position, 0, keepdims=False)
    place = jnp.concatenate([left, jnp.where(own >= 0, own, empty), right], axis=1)
    place = jnp.pad(place, ((REACH, REACH), (0, 0)), constant_values=empty)
    own_map = lax.dynamic_index_in_dim(held, position, 0, keepdims=False)
    own_count = lax.dynamic_index_in_dim(valid_count, position, 0, keepdims=False)
    head = jnp.stack([odd.astype(jnp.int32), own_count])
    return jnp.concatenate([place.reshape(-1), head, offsets.reshape(-1), own_map, near_list, far_list]), few


def finish_few(operands, near_pairs, far_pairs, tile_width, offsets):
    info, own, near_a, _, far_a, _ = operands
    far = lax.ppermute(far_a, "tm", far_pairs)
    near = lax.ppermute(near_a, "tm", near_pairs)
    part, scale, listed = inside(info, own, tile_width, offsets)
    return across(listed, scale, own, near, far, part)


def finish_many(operands, near_pairs, far_pairs, tile_width, offsets):
    info, own, near_a, near_b, far_a, far_b = operands
    far = lax.ppermute(jnp.concatenate([far_a, far_b]), "tm", far_pairs)
    near = lax.ppermute(jnp.concatenate([near_a, near_b]), "tm", near_pairs)
    part, scale, listed = inside(info, own, tile_width, offsets)
    return across(listed, scale, own, near, far, part)


def per_device(frames, frame_valid, valid_count, block_map, offsets):
    devices = lax.axis_size("tm")
    position = lax.axis_index("tm")
    frame_dev = frames.shape[0]
    frames_len = frame_dev * devices
    tile_pix = block_map.shape[1]
    slots = tile_pix // 2
    tile_width = tile_pix // ROWS
    sent = compact(frames, frame_valid, valid_count, block_map)
    tile_frames = lax.all_to_all(sent, "tm", split_axis=0, concat_axis=0, tiled=True)
    if frame_dev // RADIX % 16 != 0:
        tile_frames = tile_frames.reshape(devices, RADIX, frame_dev // RADIX, slots)
        tile_frames = tile_frames.transpose(1, 0, 2, 3).reshape(RADIX, frames_len // RADIX, slots)
    info, few = describe(valid_count, block_map, offsets, position)
    outs = transform(info, tile_frames, slots, frames_len)
    far_pairs = [(i, i + 1) for i in range(1, devices - 1, 2)] + [(i + 1, i) for i in range(1, devices - 1, 2)]
    near_pairs = [(i, i + 1) for i in range(0, devices - 1, 2)] + [(i + 1, i) for i in range(0, devices - 1, 2)]
    settings = dict(near_pairs=near_pairs, far_pairs=far_pairs, tile_width=tile_width, offsets=offsets.shape[0])
    result = lax.cond(
        few, functools.partial(finish_few, **settings), functools.partial(finish_many, **settings), (info, *outs)
    )
    bins = frames_len // 2
    result = result.reshape(tile_width, offsets.shape[0], bins // LANES, 2, LANES)
    return result.transpose(0, 1, 3, 2, 4).reshape(tile_width, offsets.shape[0], 2, bins)


def solution(mesh):
    return jax.shard_map(
        per_device,
        mesh=mesh,
        in_specs=(P("tm", "groups"), P(("groups", "tm")), P("groups"), P("groups", None), P()),
        out_specs=P(("groups", "tm"), None, None, None),
        check_vma=False,
    )
```

```python
import functools
import math

import jax
import jax.numpy as jnp
import numpy as np
from jax import lax
from jax.experimental import pallas as pl
from jax.experimental.pallas import tpu as pltpu
from jax.sharding import PartitionSpec as P

ROWS = 16
REACH = 4
RADIX = 16
LANES = 128
OFFSETS = 4
FIELDS = 8
PART = 512
CAPS = (20, 24, 32)
LANES_OF_PAIRS = 2


def dft_tables(frames_len):
    inner = frames_len // RADIX
    steps = np.arange(inner)
    angles = 2.0 * np.pi * (np.outer(steps, steps) % inner) / inner
    table = np.concatenate([np.cos(angles), -np.sin(angles)], axis=1) / math.sqrt(frames_len)
    turns = 2.0 * np.pi * np.outer(np.arange(RADIX), steps) / frames_len
    twiddle = np.stack([np.cos(turns), -np.sin(turns)], axis=1)
    twiddle = np.broadcast_to(twiddle[:, :, None, :], (RADIX, 2, 8, inner))
    return jnp.asarray(table, jnp.bfloat16), jnp.asarray(twiddle, jnp.float32)


def compact_kernel(count_hbm, valid_hbm, map_hbm, frames_hbm, out_hbm, frames, out_ref, keep, rows, count_ref, valid_ref, map_ref, sems, out_sems, small_sems):
    tile_count, frame_dev, slots = out_ref.shape
    tile_pix = map_ref.shape[1]
    batch = frames.shape[2] // tile_pix
    per_phase = frame_dev // RADIX
    pitch = RADIX + 1
    copies = []
    for step in range(frames.shape[0]):
        span = pl.ds(step * batch * tile_pix, batch * tile_pix)
        copies.append(pltpu.make_async_copy(frames_hbm.at[:, span], frames.at[step], sems.at[step]))
        copies[-1].start()
    smalls = [
        pltpu.make_async_copy(valid_hbm, valid_ref, small_sems.at[0]),
        pltpu.make_async_copy(map_hbm, map_ref, small_sems.at[1]),
        pltpu.make_async_copy(count_hbm, count_ref, small_sems.at[2]),
    ]
    for small in smalls:
        small.start()
    for small in smalls:
        small.wait()
    row = lax.broadcasted_iota(jnp.int32, (frame_dev, frame_dev), 0)
    col = lax.broadcasted_iota(jnp.int32, (frame_dev, frame_dev), 1)
    source = row % per_phase * RADIX + row // per_phase
    usable = jnp.broadcast_to(valid_ref[...], (frame_dev, frame_dev))
    order = jnp.where(col == source, usable, 0).astype(jnp.float32).astype(jnp.bfloat16)
    ones = jnp.ones((frame_dev, slots), jnp.bfloat16)
    keep[...] = jnp.dot(order, ones, preferred_element_type=jnp.float32)
    pixel = lax.broadcasted_iota(jnp.int32, (tile_pix, slots), 0)
    slot = lax.broadcasted_iota(jnp.int32, (1, slots), 1)

    def one_tile(step, which):
        tile = step * batch + which
        held = jnp.where(slot < count_ref[tile], map_ref[tile : tile + 1, :slots], -1)
        hot = jnp.where(jnp.broadcast_to(held, (tile_pix, slots)) == pixel, 1.0, 0.0).astype(jnp.bfloat16)
        block = frames[step, :, which * tile_pix : (which + 1) * tile_pix]
        picked = jnp.dot(block, hot, preferred_element_type=jnp.float32)
        for part in range(per_phase):
            rows[which, pl.ds(part * pitch, RADIX), :] = picked[part * RADIX : (part + 1) * RADIX, :]
        for phase in range(RADIX):
            span = pl.ds(phase * per_phase, per_phase)
            taken = rows[which, pl.ds(phase, per_phase, stride=pitch), :] * keep[span, :]
            out_ref[tile, span, :] = taken.astype(jnp.bfloat16)

    for step, copy in enumerate(copies):
        copy.wait()
        for which in range(batch):
            one_tile(step, which)
        span = pl.ds(step * batch, batch)
        copies[step] = pltpu.make_async_copy(out_ref.at[span], out_hbm.at[span], out_sems.at[step])
        copies[step].start()
    for copy in copies:
        copy.wait()


def compact(frames, frame_valid, valid_count, block_map):
    frame_dev, pixel_count = frames.shape
    tile_count, tile_pix = block_map.shape
    slots = tile_pix // 2
    batch = 4
    steps = tile_count // batch
    place = pl.BlockSpec(memory_space=pl.ANY)
    return pl.pallas_call(
        compact_kernel,
        name="compact",
        out_shape=jax.ShapeDtypeStruct((tile_count, frame_dev, slots), jnp.bfloat16),
        in_specs=[place] * 4,
        out_specs=place,
        scratch_shapes=[
            pltpu.VMEM((steps, frame_dev, batch * tile_pix), jnp.bfloat16),
            pltpu.VMEM((tile_count, frame_dev, slots), jnp.bfloat16),
            pltpu.VMEM((frame_dev, slots), jnp.float32),
            pltpu.VMEM((batch, frame_dev // RADIX * (RADIX + 1) + 7, slots), jnp.float32),
            pltpu.SMEM((tile_count,), jnp.int32),
            pltpu.VMEM((1, frame_dev), jnp.int32),
            pltpu.VMEM((tile_count, tile_pix), jnp.int32),
            pltpu.SemaphoreType.DMA((steps,)),
            pltpu.SemaphoreType.DMA((steps,)),
            pltpu.SemaphoreType.DMA((3,)),
        ],
        compiler_params=pltpu.CompilerParams(vmem_limit_bytes=62 * 2**20),
    )(valid_count, frame_valid.reshape(1, frame_dev), block_map, frames)


def rotate(real, imag, cos, sin):
    return real * cos - imag * sin, real * sin + imag * cos


def four_point(values):
    (r0, i0), (r1, i1), (r2, i2), (r3, i3) = values
    er, ei, fr, fi = r0 + r2, i0 + i2, r0 - r2, i0 - i2
    gr, gi, hr, hi = r1 + r3, i1 + i3, r1 - r3, i1 - i3
    return [(er + gr, ei + gi), (fr + hi, fi - hr), (er - gr, ei - gi), (fr - hi, fi + hr)]


def sixteen_point_low(values):
    inner = [four_point([values[4 * n + m] for n in range(4)]) for m in range(4)]
    low = [None] * 8
    for k in range(4):
        parts = []
        for m in range(4):
            real, imag = inner[m][k]
            turn = m * k % 16
            if turn == 0:
                parts.append((real, imag))
            elif turn == 4:
                parts.append((imag, -real))
            else:
                angle = -2.0 * math.pi * turn / 16
                parts.append(rotate(real, imag, math.cos(angle), math.sin(angle)))
        (r0, i0), (r1, i1), (r2, i2), (r3, i3) = parts
        low[k] = ((r0 + r2) + (r1 + r3), (i0 + i2) + (i1 + i3))
        low[k + 4] = ((r0 - r2) + (i1 - i3), (i0 - i2) - (r1 - r3))
    return low


def transform_kernel(send_ref, frames_ref, table_ref, twiddle_ref, own_ref, *rest):
    (edges, (phases, spread)) = rest[:-2], rest[-2:]
    slots = own_ref.shape[0] - 1
    rows = own_ref.shape[1]
    pitch = rows + 1
    half = rows // 2
    inner = table_ref.shape[0]
    edge = ROWS * REACH
    for phase in range(RADIX):
        if len(frames_ref.shape) == 3:
            per_phase = frames_ref.shape[1] // RADIX
            block = frames_ref[:, phase * per_phase : (phase + 1) * per_phase, :].reshape(inner, slots)
        else:
            block = frames_ref[phase].reshape(inner, slots)
        phases[phase] = lax.dot_general(
            block, table_ref[...], (((0,), (0,)), ((), ())), preferred_element_type=jnp.float32
        )
    groups = (send_ref[2 * (edge + 1)] + 7) // 8
    chunks = inner // LANES

    def one_group(group, carry):
        first = pl.multiple_of(group * 8, 8)
        for chunk in range(chunks):
            lanes = pl.ds(chunk * LANES, LANES)
            values = []
            for phase in range(RADIX):
                real = phases[phase, pl.ds(first, 8), lanes]
                imag = phases[phase, pl.ds(first, 8), pl.ds(inner + chunk * LANES, LANES)]
                if phase > 0:
                    real, imag = rotate(real, imag, twiddle_ref[phase, 0, :, lanes], twiddle_ref[phase, 1, :, lanes])
                values.append((real, imag))
            for high, (real, imag) in enumerate(sixteen_point_low(values)):
                at = first * pitch + high * chunks + chunk
                spread[pl.ds(at, 8, stride=pitch), :] = real
                spread[pl.ds(at + half, 8, stride=pitch), :] = imag
        return carry

    lax.fori_loop(0, groups, one_group, 0)

    def eight_slots(group, carry):
        for slot in range(8):
            slot = group * 8 + slot
            own_ref[slot] = spread[pl.ds(slot * pitch, rows), :].astype(jnp.bfloat16)
        return carry

    lax.fori_loop(0, groups, eight_slots, 0)
    own_ref[slots] = jnp.zeros((rows, LANES), jnp.bfloat16)
    sides = len(edges) // 2
    bounds = [0] + [ref.shape[0] for ref in edges[: sides - 1]]
    for low, high in zip(bounds[:-1], bounds[1:]):

        def one_edge(spot, carry, high=high):
            for side in range(2):
                block = own_ref[send_ref[side * (edge + 1) + spot]]
                for ref in edges[side * sides : side * sides + sides - 1]:
                    if ref.shape[0] >= high:
                        ref[spot] = block
            return carry

        lax.fori_loop(low, high, one_edge, 0, unroll=4)

    def one_rest(spot, carry):
        for side in range(2):
            ref = edges[side * sides + sides - 1]
            ref[spot] = own_ref[send_ref[side * (edge + 1) + bounds[-1] + spot]]
        return carry

    lax.fori_loop(0, edge - bounds[-1], one_rest, 0, unroll=4)


def transform(send, tile_frames, slots, frames_len):
    table, twiddle = dft_tables(frames_len)
    inner = frames_len // RADIX
    rows = frames_len // LANES
    edge = ROWS * REACH
    sizes = [*CAPS, edge - CAPS[-1]] * 2
    whole = pl.BlockSpec(memory_space=pltpu.VMEM)
    return pl.pallas_call(
        transform_kernel,
        name="transform",
        out_shape=(
            jax.ShapeDtypeStruct((slots + 1, rows, LANES), jnp.bfloat16),
            *[jax.ShapeDtypeStruct((size, rows, LANES), jnp.bfloat16) for size in sizes],
        ),
        in_specs=[pl.BlockSpec(memory_space=pltpu.SMEM), whole, whole, whole],
        out_specs=(whole,) * (1 + len(sizes)),
        scratch_shapes=[
            pltpu.VMEM((RADIX, slots, 2 * inner), jnp.float32),
            pltpu.VMEM((slots * (rows + 1) + 7, LANES), jnp.float32),
        ],
        compiler_params=pltpu.CompilerParams(vmem_limit_bytes=24 * 2**20),
    )(send, tile_frames, table, twiddle)


def unpacked(code):
    return code % PART, code // PART % PART, code // PART // PART


def cross_terms(first, second):
    half = first.shape[0] // 2
    first = first.astype(jnp.float32)
    second = second.astype(jnp.float32)
    own_real, own_imag = first[:half], first[half:]
    real, imag = second[:half], second[half:]
    return own_real * real + own_imag * imag, own_imag * real - own_real * imag


def inside_kernel(slot_ref, list_ref, scale_ref, own_ref, near_ref, out_hbm, border_ref, result, sem, *totals):
    slots, rows = own_ref.shape[0] - 1, own_ref.shape[1]
    half = rows // 2
    offsets = len(totals)
    for total in totals:
        total[...] = jnp.zeros(total.shape, jnp.float32)

    def one_slot(slot, carry):
        column = slot_ref[slot * FIELDS]
        own = own_ref[slot]
        for j, total in enumerate(totals):
            real, imag = cross_terms(own, own_ref[slot_ref[slot * FIELDS + 1 + j]])
            total[column, :half] += real
            total[column, half:] += imag
        return carry

    lax.fori_loop(0, slot_ref[slots * FIELDS], one_slot, 0)
    for column in range(totals[0].shape[0]):
        for j, total in enumerate(totals):
            at = column * offsets + j
            scaling = scale_ref[j, column]
            result[at, pl.ds(0, half, stride=2), :] = total[column, :half] * scaling
            result[at, pl.ds(1, half, stride=2), :] = total[column, half:] * scaling

    def one_pair(pair, carry):
        slot, other, at = unpacked(list_ref[pair])
        real, imag = cross_terms(own_ref[slot], near_ref[other - slots])
        scaling = scale_ref[at % offsets, at // offsets]
        result[at, pl.ds(0, half, stride=2), :] += real * scaling
        result[at, pl.ds(1, half, stride=2), :] += imag * scaling
        return carry

    lax.fori_loop(0, slot_ref[slots * FIELDS + 1], one_pair, 0)
    copy = pltpu.make_async_copy(result, out_hbm, sem)
    copy.start()
    base = slot_ref[slots * FIELDS + 2]
    for spot in range(2 * REACH):
        border_ref[spot] = result[base + spot // 2 * offsets + spot % 2]
    copy.wait()


def inside(slot_info, near_pairs, scale, own, near, tile_width, offsets):
    rows = own.shape[1]
    spots = tile_width * offsets
    small = pl.BlockSpec(memory_space=pltpu.SMEM)
    whole = pl.BlockSpec(memory_space=pltpu.VMEM)
    return pl.pallas_call(
        inside_kernel,
        name="inside",
        out_shape=(
            pltpu.HBM((spots, rows, LANES), jnp.float32),
            jax.ShapeDtypeStruct((2 * REACH, rows, LANES), jnp.float32),
        ),
        in_specs=[small, small, small, whole, whole],
        out_specs=(pl.BlockSpec(memory_space=pl.ANY), whole),
        scratch_shapes=[pltpu.VMEM((spots, rows, LANES), jnp.float32), pltpu.SemaphoreType.DMA]
        + [pltpu.VMEM((tile_width, rows, LANES), jnp.float32)] * offsets,
        compiler_params=pltpu.CompilerParams(vmem_limit_bytes=16 * 2**20),
        cost_estimate=pl.CostEstimate(flops=60_000_000, bytes_accessed=4_000_000, transcendentals=0),
    )(slot_info, near_pairs, scale, own, near)


def across_kernel(slot_ref, list_ref, scale_ref, own_ref, far_ref, border_ref, part_hbm, out_hbm, result, sem, *totals):
    del part_hbm
    slots, rows = own_ref.shape[0] - 1, own_ref.shape[1]
    half = rows // 2
    first_far = slots + ROWS * REACH
    offsets = scale_ref.shape[0] // 2
    base = slot_ref[slots * FIELDS + 2]
    for total in totals:
        total[...] = jnp.zeros(total.shape, jnp.float32)

    def some_pairs(group, carry):
        for which, total in enumerate(totals):
            slot, other, at = unpacked(list_ref[group * len(totals) + which])
            spot = (at - base) // offsets * 2 + (at - base) % offsets
            real, imag = cross_terms(own_ref[slot], far_ref[other - first_far])
            total[spot, :half] += real
            total[spot, half:] += imag
        return carry

    pairs = slot_ref[slots * FIELDS + 3]
    lax.fori_loop(0, (pairs + len(totals) - 1) // len(totals), some_pairs, 0)
    copies = []
    for column in range(REACH):
        for j in range(2):
            spot = 2 * column + j
            at = base + column * offsets + j
            scaling = scale_ref[at % offsets, at // offsets]
            total = totals[0][spot]
            for other in totals[1:]:
                total = total + other[spot]
            total = total * scaling
            result[spot, pl.ds(0, half, stride=2), :] = border_ref[spot, pl.ds(0, half, stride=2), :] + total[:half]
            result[spot, pl.ds(1, half, stride=2), :] = border_ref[spot, pl.ds(1, half, stride=2), :] + total[half:]
        copies.append(
            pltpu.make_async_copy(
                result.at[pl.ds(2 * column, 2)], out_hbm.at[pl.ds(base + column * offsets, 2)], sem.at[column]
            )
        )
        copies[-1].start()
    for copy in copies:
        copy.wait()


def across(slot_info, far_pairs, scale, own, far, border, part):
    rows = own.shape[1]
    small = pl.BlockSpec(memory_space=pltpu.SMEM)
    whole = pl.BlockSpec(memory_space=pltpu.VMEM)
    place = pl.BlockSpec(memory_space=pl.ANY)
    return pl.pallas_call(
        across_kernel,
        name="across",
        out_shape=pltpu.HBM(part.shape, part.dtype),
        in_specs=[small, small, small, whole, whole, whole, place],
        out_specs=place,
        scratch_shapes=[pltpu.VMEM((2 * REACH, rows, LANES), jnp.float32), pltpu.SemaphoreType.DMA((REACH,))]
        + [pltpu.VMEM((2 * REACH, rows, LANES), jnp.float32)] * LANES_OF_PAIRS,
        input_output_aliases={6: 0},
        compiler_params=pltpu.CompilerParams(vmem_limit_bytes=16 * 2**20),
    )(slot_info, far_pairs, scale, own, far, border, part)


def plan_kernel(offset_ref, position_ref, count_ref, map_ref, table_ref, scale_ref, level_ref):
    tile_count, pixels = map_ref.shape
    slots = pixels // 2
    tile_width = pixels // ROWS
    edge = ROWS * REACH
    empty = slots + 2 * edge
    position = position_ref[0]
    offsets = [(offset_ref[j, 0], offset_ref[j, 1]) for j in range(offset_ref.shape[0])]
    held = jnp.where(
        lax.broadcasted_iota(jnp.int32, (tile_count, slots), 1) < count_ref[...], map_ref[:, :slots], -1
    )
    pixel = lax.broadcasted_iota(jnp.int32, (tile_count, pixels), 1)
    tile = lax.broadcasted_iota(jnp.int32, (tile_count, pixels), 0)
    row = pixel // tile_width
    column = pixel % tile_width
    found = jnp.zeros((tile_count, pixels), jnp.int32)
    for slot in range(slots):
        found = jnp.where(held[:, slot : slot + 1] == pixel, slot + 1, found)
    valid = jnp.where(found > 0, 1, 0)
    left_valid = jnp.where(tile > 0, pltpu.roll(valid, 1, 0), 0)
    right_valid = jnp.where(tile < tile_count - 1, pltpu.roll(valid, tile_count - 1, 0), 0)

    def turned(values, shift):
        return pltpu.roll(values, lax.rem(shift + 2 * pixels, pixels), 1)

    for_left = jnp.zeros((tile_count, pixels), jnp.int32)
    for_right = jnp.zeros((tile_count, pixels), jnp.int32)
    for down, across_by in offsets:
        shift = down * tile_width + across_by
        inside_rows = (row >= down) & (row < ROWS + down)
        partner = turned(left_valid, shift - tile_width)
        for_left = jnp.where(inside_rows & (column < across_by), jnp.maximum(for_left, partner), for_left)
        partner = turned(right_valid, shift + tile_width)
        for_right = jnp.where(
            inside_rows & (column >= tile_width + across_by), jnp.maximum(for_right, partner), for_right
        )
    before = jnp.where(
        lax.broadcasted_iota(jnp.int32, (pixels, pixels), 0) <= lax.broadcasted_iota(jnp.int32, (pixels, pixels), 1),
        1.0,
        0.0,
    ).astype(jnp.bfloat16)

    def numbered(needed):
        needed = (needed * valid).astype(jnp.float32)
        ranks = jnp.dot(needed.astype(jnp.bfloat16), before, preferred_element_type=jnp.float32) * needed
        return ranks.astype(jnp.int32), jnp.max(ranks)

    left_rank, left_most = numbered(for_left)
    right_rank, right_most = numbered(for_right)
    most = jnp.maximum(left_most, right_most)
    level_ref[0] = sum([jnp.where(most <= cap, 0, 1) for cap in CAPS])

    def chosen(values, which):
        picked = jnp.sum(jnp.where(tile == which, values, 0), axis=0, keepdims=True)
        return jnp.broadcast_to(picked, (8, pixels))

    odd = lax.rem(position, 2)
    row, column = row[:8], column[:8]
    own = chosen(found, position)
    right = chosen(left_rank, position + 1)
    left = chosen(right_rank, position - 1)
    own_place = jnp.where(own > 0, own - 1, empty)
    right_place = jnp.where(right > 0, slots + odd * edge - 1 + right, empty)
    left_place = jnp.where(left > 0, slots + (1 - odd) * edge - 1 + left, empty)
    selector = jnp.where(
        lax.broadcasted_iota(jnp.int32, (pixels, LANES), 0) % tile_width
        == lax.broadcasted_iota(jnp.int32, (pixels, LANES), 1),
        1.0,
        0.0,
    ).astype(jnp.bfloat16)
    spot = lax.broadcasted_iota(jnp.int32, (8, pixels), 0)
    seen = jnp.zeros((8, pixels), jnp.float32)
    table = jnp.zeros((8, pixels), jnp.int32)
    for j, (down, across_by) in enumerate(offsets):
        shift = down * tile_width + across_by
        other = turned(own_place, -shift)
        other = jnp.where(column + across_by < 0, turned(left_place, -shift - tile_width), other)
        other = jnp.where(column + across_by >= tile_width, turned(right_place, tile_width - shift), other)
        other = jnp.where((row + down >= 0) & (row + down < ROWS), other, empty)
        seen = jnp.where((spot == j) & (own > 0) & (other < empty), 1.0, seen)
        table = jnp.where(spot == j, other, table)
    own_left = chosen(left_rank, position)
    own_right = chosen(right_rank, position)
    near = jnp.where(odd == 1, own_left, own_right)
    far = jnp.where(odd == 1, own_right, own_left)
    table = jnp.where(spot == len(offsets), jnp.where(near > 0, near - 1, edge), table)
    table = jnp.where(spot == len(offsets) + 1, jnp.where(far > 0, far - 1, edge), table)
    wide = jnp.concatenate([held, held], axis=1)
    table_ref[...] = jnp.where(spot == len(offsets) + 2, chosen(wide, position), table)
    pairs = jnp.dot(seen.astype(jnp.bfloat16), selector, preferred_element_type=jnp.float32)
    scale_ref[...] = 1.0 / jnp.maximum(pairs, 1.0)


def listing_kernel(table_ref, count_ref, position_ref, slot_ref, send_ref, near_ref, far_ref):
    slots = table_ref.shape[1] // 2
    tile_width = table_ref.shape[1] // ROWS
    edge = ROWS * REACH
    empty = slots + 2 * edge
    position = position_ref[0]
    count = count_ref[position]
    odd = lax.rem(position, 2)

    def clear(spot, carry):
        send_ref[spot] = 0
        return carry

    lax.fori_loop(0, 2 * (edge + 1), clear, 0, unroll=10)

    def one_slot(slot, listed):
        close, distant = listed
        pixel = table_ref[OFFSETS + 2, slot]
        column = pixel % tile_width
        slot_ref[slot * FIELDS] = column
        send_ref[table_ref[OFFSETS, pixel]] = slot
        send_ref[edge + 1 + table_ref[OFFSETS + 1, pixel]] = slot
        for j in range(OFFSETS):
            other = table_ref[j, pixel]
            slot_ref[slot * FIELDS + 1 + j] = jnp.minimum(other, slots)
            code = ((column * OFFSETS + j) * PART + other) * PART + slot
            near_ref[close] = code
            far_ref[distant] = code
            close = close + jnp.where((other >= slots) & (other < slots + edge), 1, 0)
            distant = distant + jnp.where((other >= slots + edge) & (other < empty), 1, 0)
        return close, distant

    close, distant = lax.fori_loop(0, count, one_slot, (0, 0))
    base = jnp.where(odd == 1, (tile_width - REACH) * OFFSETS, OFFSETS // 2)
    for spare in range(LANES_OF_PAIRS - 1):
        far_ref[distant + spare] = (base * PART + slots + edge) * PART + slots
    send_ref[2 * (edge + 1)] = count
    slot_ref[slots * FIELDS] = count
    slot_ref[slots * FIELDS + 1] = close
    slot_ref[slots * FIELDS + 2] = base
    slot_ref[slots * FIELDS + 3] = distant


def plan(valid_count, block_map, offsets, position):
    tile_count, pixels = block_map.shape
    slots = pixels // 2
    small = pl.BlockSpec(memory_space=pltpu.SMEM)
    whole = pl.BlockSpec(memory_space=pltpu.VMEM)
    position = jnp.full((1,), position, jnp.int32)
    table, scale, level = pl.pallas_call(
        plan_kernel,
        name="plan",
        out_shape=(
            jax.ShapeDtypeStruct((8, pixels), jnp.int32),
            jax.ShapeDtypeStruct((8, LANES), jnp.float32),
            jax.ShapeDtypeStruct((1,), jnp.int32),
        ),
        in_specs=[small, small, whole, whole],
        out_specs=(whole, whole, small),
        compiler_params=pltpu.CompilerParams(vmem_limit_bytes=16 * 2**20),
    )(offsets, position, valid_count.reshape(tile_count, 1), block_map)
    slot_info, send, near_list, far_list = pl.pallas_call(
        listing_kernel,
        name="listing",
        out_shape=(
            jax.ShapeDtypeStruct((slots * FIELDS + 4,), jnp.int32),
            jax.ShapeDtypeStruct((2 * (ROWS * REACH + 1) + 1,), jnp.int32),
            jax.ShapeDtypeStruct((slots * OFFSETS + 1,), jnp.int32),
            jax.ShapeDtypeStruct((slots * OFFSETS + LANES_OF_PAIRS,), jnp.int32),
        ),
        in_specs=[small, small, small],
        out_specs=(small,) * 4,
        compiler_params=pltpu.CompilerParams(vmem_limit_bytes=16 * 2**20),
    )(table, valid_count, position)
    return scale, level[0], slot_info, send, near_list, far_list


def finish(level, near_pairs, far_pairs, tile_width, offsets, operands):
    slot_info, scale, near_list, far_list, own, *edges = operands
    nears, fars = edges[: len(edges) // 2], edges[len(edges) // 2 :]
    if level < len(CAPS):
        near, far = nears[level], fars[level]
    else:
        near, far = jnp.concatenate(nears[-2:]), jnp.concatenate(fars[-2:])
    far = lax.ppermute(far, "tm", far_pairs)
    near = lax.ppermute(near, "tm", near_pairs)
    part, border = inside(slot_info, near_list, scale, own, near, tile_width, offsets)
    result = across(slot_info, far_list, scale, own, far, border, part)
    groups = result.shape[1] // 2
    result = result.reshape(tile_width, offsets, groups, 2, LANES)
    return result.transpose(0, 1, 3, 2, 4).reshape(tile_width, offsets, 2, groups * LANES)


def per_device(frames, frame_valid, valid_count, block_map, offsets):
    devices = lax.axis_size("tm")
    position = lax.axis_index("tm")
    frame_dev = frames.shape[0]
    frames_len = frame_dev * devices
    tile_pix = block_map.shape[1]
    slots = tile_pix // 2
    tile_width = tile_pix // ROWS
    sent = compact(frames, frame_valid, valid_count, block_map)
    tile_frames = lax.all_to_all(sent, "tm", split_axis=0, concat_axis=0, tiled=True)
    if frame_dev // RADIX % 16 != 0:
        tile_frames = tile_frames.reshape(devices, RADIX, frame_dev // RADIX, slots)
        tile_frames = tile_frames.transpose(1, 0, 2, 3).reshape(RADIX, frames_len // RADIX, slots)
    scale, level, slot_info, send, near_list, far_list = plan(valid_count, block_map, offsets, position)
    outs = transform(send, tile_frames, slots, frames_len)
    far_pairs = [(i, i + 1) for i in range(1, devices - 1, 2)] + [(i + 1, i) for i in range(1, devices - 1, 2)]
    near_pairs = [(i, i + 1) for i in range(0, devices - 1, 2)] + [(i + 1, i) for i in range(0, devices - 1, 2)]
    branches = [
        functools.partial(finish, which, near_pairs, far_pairs, tile_width, offsets.shape[0])
        for which in range(len(CAPS) + 1)
    ]
    return lax.switch(level, branches, (slot_info, scale, near_list, far_list, *outs))


def solution(mesh):
    return jax.shard_map(
        per_device,
        mesh=mesh,
        in_specs=(P("tm", "groups"), P(("groups", "tm")), P("groups"), P("groups", None), P()),
        out_specs=P(("groups", "tm"), None, None, None),
        check_vma=False,
    )
```

```python
import functools
import math

import jax
import jax.numpy as jnp
import numpy as np
from jax import lax
from jax.experimental import pallas as pl
from jax.experimental.pallas import tpu as pltpu
from jax.sharding import PartitionSpec as P

ROWS = 16
REACH = 4
RADIX = 16
LANES = 128
OFFSETS = 4
PART = 512
CAPS = (20, 24, 32)
LANES_OF_PAIRS = 2
PAIRED = 16


def dft_tables(frames_len):
    inner = frames_len // RADIX
    steps = np.arange(inner)
    angles = 2.0 * np.pi * (np.outer(steps, steps) % inner) / inner
    table = np.concatenate([np.cos(angles), -np.sin(angles)], axis=1) / math.sqrt(frames_len)
    turns = 2.0 * np.pi * np.outer(np.arange(RADIX), steps) / frames_len
    twiddle = np.stack([np.cos(turns), -np.sin(turns)], axis=1)
    twiddle = np.broadcast_to(twiddle[:, :, None, :], (RADIX, 2, 8, inner))
    return jnp.asarray(table, jnp.bfloat16), jnp.asarray(twiddle, jnp.float32)


def compact_kernel(count_hbm, valid_hbm, map_hbm, frames_hbm, out_hbm, frames, out_ref, keep, rows, count_ref, valid_ref, map_ref, sems, out_sems, small_sems):
    tile_count, frame_dev, slots = out_ref.shape
    tile_pix = map_ref.shape[1]
    batch = frames.shape[2] // tile_pix
    per_phase = frame_dev // RADIX
    pitch = RADIX + 1
    copies = []
    for step in range(frames.shape[0]):
        span = pl.ds(step * batch * tile_pix, batch * tile_pix)
        copies.append(pltpu.make_async_copy(frames_hbm.at[:, span], frames.at[step], sems.at[step]))
        copies[-1].start()
    smalls = [
        pltpu.make_async_copy(valid_hbm, valid_ref, small_sems.at[0]),
        pltpu.make_async_copy(map_hbm, map_ref, small_sems.at[1]),
        pltpu.make_async_copy(count_hbm, count_ref, small_sems.at[2]),
    ]
    for small in smalls:
        small.start()
    for small in smalls:
        small.wait()
    row = lax.broadcasted_iota(jnp.int32, (frame_dev, frame_dev), 0)
    col = lax.broadcasted_iota(jnp.int32, (frame_dev, frame_dev), 1)
    source = row % per_phase * RADIX + row // per_phase
    usable = jnp.broadcast_to(valid_ref[...], (frame_dev, frame_dev))
    order = jnp.where(col == source, usable, 0).astype(jnp.float32).astype(jnp.bfloat16)
    ones = jnp.ones((frame_dev, slots), jnp.bfloat16)
    keep[...] = jnp.dot(order, ones, preferred_element_type=jnp.float32)
    pixel = lax.broadcasted_iota(jnp.int32, (tile_pix, slots), 0)
    slot = lax.broadcasted_iota(jnp.int32, (1, slots), 1)

    def one_tile(step, which):
        tile = step * batch + which
        held = jnp.where(slot < count_ref[tile], map_ref[tile : tile + 1, :slots], -1)
        hot = jnp.where(jnp.broadcast_to(held, (tile_pix, slots)) == pixel, 1.0, 0.0).astype(jnp.bfloat16)
        block = frames[step, :, which * tile_pix : (which + 1) * tile_pix]
        picked = jnp.dot(block, hot, preferred_element_type=jnp.float32)
        for part in range(per_phase):
            rows[which, pl.ds(part * pitch, RADIX), :] = picked[part * RADIX : (part + 1) * RADIX, :]
        for phase in range(RADIX):
            span = pl.ds(phase * per_phase, per_phase)
            taken = rows[which, pl.ds(phase, per_phase, stride=pitch), :] * keep[span, :]
            out_ref[tile, span, :] = taken.astype(jnp.bfloat16)

    for step, copy in enumerate(copies):
        copy.wait()
        for which in range(batch):
            one_tile(step, which)
        span = pl.ds(step * batch, batch)
        copies[step] = pltpu.make_async_copy(out_ref.at[span], out_hbm.at[span], out_sems.at[step])
        copies[step].start()
    for copy in copies:
        copy.wait()


def compact(frames, frame_valid, valid_count, block_map):
    frame_dev, pixel_count = frames.shape
    tile_count, tile_pix = block_map.shape
    slots = tile_pix // 2
    batch = 4
    steps = tile_count // batch
    place = pl.BlockSpec(memory_space=pl.ANY)
    return pl.pallas_call(
        compact_kernel,
        name="compact",
        out_shape=jax.ShapeDtypeStruct((tile_count, frame_dev, slots), jnp.bfloat16),
        in_specs=[place] * 4,
        out_specs=place,
        scratch_shapes=[
            pltpu.VMEM((steps, frame_dev, batch * tile_pix), jnp.bfloat16),
            pltpu.VMEM((tile_count, frame_dev, slots), jnp.bfloat16),
            pltpu.VMEM((frame_dev, slots), jnp.float32),
            pltpu.VMEM((batch, frame_dev // RADIX * (RADIX + 1) + 7, slots), jnp.float32),
            pltpu.SMEM((tile_count,), jnp.int32),
            pltpu.VMEM((1, frame_dev), jnp.int32),
            pltpu.VMEM((tile_count, tile_pix), jnp.int32),
            pltpu.SemaphoreType.DMA((steps,)),
            pltpu.SemaphoreType.DMA((steps,)),
            pltpu.SemaphoreType.DMA((3,)),
        ],
        compiler_params=pltpu.CompilerParams(vmem_limit_bytes=62 * 2**20),
    )(valid_count, frame_valid.reshape(1, frame_dev), block_map, frames)


def send_order(devices):
    half = devices // 2
    near = list(range(1, half))
    step = half // 2
    far = [half + (i % 2) * step + i // 2 for i in range(half)]
    order = []
    for i, which in enumerate(far):
        order.append(which)
        if i < len(near):
            order.append(near[i])
    return order


def paired_kernel(group, count_hbm, valid_hbm, map_hbm, frames_hbm, *rest):
    *outs, frames, keep, rows, count_ref, valid_ref, map_ref, sems, small_sems = rest
    position = lax.axis_index("tm")
    frame_dev, slots = outs[0].shape
    tile_count, tile_pix = map_ref.shape
    per_phase = frame_dev // RADIX
    pitch = RADIX + 1
    steps = tile_count // group
    steps_order = [(step + steps // 2) % steps for step in range(steps)]
    copies = {}
    for step in steps_order:
        first = jnp.bitwise_xor(position, step * group) // group * group
        span = pl.ds(pl.multiple_of(first * tile_pix, group * tile_pix), group * tile_pix)
        copies[step] = pltpu.make_async_copy(frames_hbm.at[:, span], frames.at[step], sems.at[step])
        copies[step].start()
    smalls = [
        pltpu.make_async_copy(valid_hbm, valid_ref, small_sems.at[0]),
        pltpu.make_async_copy(map_hbm, map_ref, small_sems.at[1]),
        pltpu.make_async_copy(count_hbm, count_ref, small_sems.at[2]),
    ]
    for small in smalls:
        small.start()
    for small in smalls:
        small.wait()
    row = lax.broadcasted_iota(jnp.int32, (frame_dev, frame_dev), 0)
    col = lax.broadcasted_iota(jnp.int32, (frame_dev, frame_dev), 1)
    source = row % per_phase * RADIX + row // per_phase
    usable = jnp.broadcast_to(valid_ref[...], (frame_dev, frame_dev))
    order = jnp.where(col == source, usable, 0).astype(jnp.float32).astype(jnp.bfloat16)
    ones = jnp.ones((frame_dev, slots), jnp.bfloat16)
    keep[...] = jnp.dot(order, ones, preferred_element_type=jnp.float32)
    pixel = lax.broadcasted_iota(jnp.int32, (tile_pix, slots), 0)
    slot = lax.broadcasted_iota(jnp.int32, (1, slots), 1)
    tiles = lax.broadcasted_iota(jnp.int32, (tile_count, slots), 0)
    for step in steps_order:
        copies[step].wait()
        for which in range(group):
            out_ref = outs[step * group + which]
            tile = jnp.bitwise_xor(position, step * group + which)
            held = jnp.sum(jnp.where(tiles == tile, map_ref[:, :slots], 0), axis=0, keepdims=True)
            held = jnp.where(slot < count_ref[tile], held, -1)
            hot = jnp.where(jnp.broadcast_to(held, (tile_pix, slots)) == pixel, 1.0, 0.0).astype(jnp.bfloat16)
            block = frames[step, :, pl.ds(pl.multiple_of(tile % group * tile_pix, tile_pix), tile_pix)]
            picked = jnp.dot(block, hot, preferred_element_type=jnp.float32)
            for part in range(per_phase):
                rows[which, pl.ds(part * pitch, RADIX), :] = picked[part * RADIX : (part + 1) * RADIX, :]
            for phase in range(RADIX):
                span = pl.ds(phase * per_phase, per_phase)
                taken = rows[which, pl.ds(phase, per_phase, stride=pitch), :] * keep[span, :]
                out_ref[span, :] = taken.astype(jnp.bfloat16)


def compact_paired(frames, frame_valid, valid_count, block_map):
    frame_dev, pixel_count = frames.shape
    tile_count, tile_pix = block_map.shape
    slots = tile_pix // 2
    group = 4
    steps = tile_count // group
    place = pl.BlockSpec(memory_space=pl.ANY)
    return pl.pallas_call(
        functools.partial(paired_kernel, group),
        name="compact",
        out_shape=[jax.ShapeDtypeStruct((frame_dev, slots), jnp.bfloat16)] * tile_count,
        in_specs=[place] * 4,
        out_specs=[pl.BlockSpec(memory_space=pltpu.VMEM)] * tile_count,
        scratch_shapes=[
            pltpu.VMEM((steps, frame_dev, group * tile_pix), jnp.bfloat16),
            pltpu.VMEM((frame_dev, slots), jnp.float32),
            pltpu.VMEM((group, frame_dev // RADIX * (RADIX + 1) + 7, slots), jnp.float32),
            pltpu.SMEM((tile_count,), jnp.int32),
            pltpu.VMEM((1, frame_dev), jnp.int32),
            pltpu.VMEM((tile_count, tile_pix), jnp.int32),
            pltpu.SemaphoreType.DMA((steps,)),
            pltpu.SemaphoreType.DMA((3,)),
        ],
        compiler_params=pltpu.CompilerParams(vmem_limit_bytes=16 * 2**20),
    )(
        pltpu.with_memory_space_constraint(valid_count, pltpu.HBM),
        pltpu.with_memory_space_constraint(frame_valid.reshape(1, frame_dev), pltpu.HBM),
        pltpu.with_memory_space_constraint(block_map, pltpu.HBM),
        pltpu.with_memory_space_constraint(frames, pltpu.HBM),
    )


def turn_kernel(order, position_ref, table_ref, out_ref):
    per_phase = table_ref.shape[0] // len(order)
    for place, which in enumerate(order):
        source = jnp.bitwise_xor(position_ref[0], which)
        rows = pl.ds(pl.multiple_of(source * per_phase, per_phase), per_phase)
        out_ref[pl.ds(place * per_phase, per_phase), :] = table_ref[rows, :]


def turn_table(table, position, order):
    whole = pl.BlockSpec(memory_space=pltpu.VMEM)
    return pl.pallas_call(
        functools.partial(turn_kernel, order),
        name="turn",
        out_shape=jax.ShapeDtypeStruct(table.shape, table.dtype),
        in_specs=[pl.BlockSpec(memory_space=pltpu.SMEM), whole],
        out_specs=whole,
        compiler_params=pltpu.CompilerParams(vmem_limit_bytes=16 * 2**20),
    )(jnp.full((1,), position, jnp.int32), table)


def rotate(real, imag, cos, sin):
    return real * cos - imag * sin, real * sin + imag * cos


def four_point(values):
    (r0, i0), (r1, i1), (r2, i2), (r3, i3) = values
    er, ei, fr, fi = r0 + r2, i0 + i2, r0 - r2, i0 - i2
    gr, gi, hr, hi = r1 + r3, i1 + i3, r1 - r3, i1 - i3
    return [(er + gr, ei + gi), (fr + hi, fi - hr), (er - gr, ei - gi), (fr - hi, fi + hr)]


def sixteen_point_low(values):
    inner = [four_point([values[4 * n + m] for n in range(4)]) for m in range(4)]
    low = [None] * 8
    for k in range(4):
        parts = []
        for m in range(4):
            real, imag = inner[m][k]
            turn = m * k % 16
            if turn == 0:
                parts.append((real, imag))
            elif turn == 4:
                parts.append((imag, -real))
            else:
                angle = -2.0 * math.pi * turn / 16
                parts.append(rotate(real, imag, math.cos(angle), math.sin(angle)))
        (r0, i0), (r1, i1), (r2, i2), (r3, i3) = parts
        low[k] = ((r0 + r2) + (r1 + r3), (i0 + i2) + (i1 + i3))
        low[k + 4] = ((r0 - r2) + (i1 - i3), (i0 - i2) - (r1 - r3))
    return low


def transform_kernel(blocks, send_ref, table_ref, twiddle_ref, *rest):
    frames, own_ref = rest[:blocks], rest[blocks]
    edges, (phases, spread) = rest[blocks + 1 : -2], rest[-2:]
    slots = own_ref.shape[0] - 1
    rows = own_ref.shape[1]
    pitch = rows + 1
    half = rows // 2
    inner = table_ref.shape[0]
    edge = ROWS * REACH
    for phase in range(RADIX):
        if blocks > 1:
            per_phase = inner // blocks
            span = slice(phase * per_phase, (phase + 1) * per_phase)
            block = jnp.concatenate([ref[span, :] for ref in frames], axis=0)
        elif frames[0].shape[0] != RADIX:
            per_phase = frames[0].shape[1] // RADIX
            block = frames[0][:, phase * per_phase : (phase + 1) * per_phase, :].reshape(inner, slots)
        else:
            block = frames[0][phase].reshape(inner, slots)
        phases[phase] = lax.dot_general(
            block, table_ref[...], (((0,), (0,)), ((), ())), preferred_element_type=jnp.float32
        )
    groups = (send_ref[2 * (edge + 1)] + 7) // 8
    chunks = inner // LANES

    def one_group(group, carry):
        first = pl.multiple_of(group * 8, 8)
        for chunk in range(chunks):
            lanes = pl.ds(chunk * LANES, LANES)
            values = []
            for phase in range(RADIX):
                real = phases[phase, pl.ds(first, 8), lanes]
                imag = phases[phase, pl.ds(first, 8), pl.ds(inner + chunk * LANES, LANES)]
                if phase > 0:
                    real, imag = rotate(real, imag, twiddle_ref[phase, 0, :, lanes], twiddle_ref[phase, 1, :, lanes])
                values.append((real, imag))
            for high, (real, imag) in enumerate(sixteen_point_low(values)):
                at = first * pitch + high * chunks + chunk
                spread[pl.ds(at, 8, stride=pitch), :] = real
                spread[pl.ds(at + half, 8, stride=pitch), :] = imag
        return carry

    lax.fori_loop(0, groups, one_group, 0)

    def eight_slots(group, carry):
        for slot in range(8):
            slot = group * 8 + slot
            own_ref[slot] = spread[pl.ds(slot * pitch, rows), :].astype(jnp.bfloat16)
        return carry

    lax.fori_loop(0, groups, eight_slots, 0)
    own_ref[slots] = jnp.zeros((rows, LANES), jnp.bfloat16)
    sides = len(edges) // 2
    bounds = [0] + [ref.shape[0] for ref in edges[: sides - 1]]
    for low, high in zip(bounds[:-1], bounds[1:]):

        def one_edge(spot, carry, high=high):
            for side in range(2):
                block = own_ref[send_ref[side * (edge + 1) + spot]]
                for ref in edges[side * sides : side * sides + sides - 1]:
                    if ref.shape[0] >= high:
                        ref[spot] = block
            return carry

        lax.fori_loop(low, high, one_edge, 0, unroll=4)

    def one_rest(spot, carry):
        for side in range(2):
            ref = edges[side * sides + sides - 1]
            ref[spot] = own_ref[send_ref[side * (edge + 1) + bounds[-1] + spot]]
        return carry

    lax.fori_loop(0, edge - bounds[-1], one_rest, 0, unroll=4)


def transform(send, table, twiddle, tile_frames, slots, frames_len):
    inner = frames_len // RADIX
    rows = frames_len // LANES
    edge = ROWS * REACH
    sizes = [*CAPS, edge - CAPS[-1]] * 2
    whole = pl.BlockSpec(memory_space=pltpu.VMEM)
    return pl.pallas_call(
        functools.partial(transform_kernel, len(tile_frames)),
        name="transform",
        out_shape=(
            jax.ShapeDtypeStruct((slots + 1, rows, LANES), jnp.bfloat16),
            *[jax.ShapeDtypeStruct((size, rows, LANES), jnp.bfloat16) for size in sizes],
        ),
        in_specs=[pl.BlockSpec(memory_space=pltpu.SMEM)] + [whole] * (2 + len(tile_frames)),
        out_specs=(whole,) * (1 + len(sizes)),
        scratch_shapes=[
            pltpu.VMEM((RADIX, slots, 2 * inner), jnp.float32),
            pltpu.VMEM((slots * (rows + 1) + 7, LANES), jnp.float32),
        ],
        compiler_params=pltpu.CompilerParams(vmem_limit_bytes=24 * 2**20),
    )(send, table, twiddle, *tile_frames)


def unpacked(code):
    return code % PART, code // PART % PART, code // PART // PART


def cross_terms(first, second):
    half = first.shape[0] // 2
    first = first.astype(jnp.float32)
    second = second.astype(jnp.float32)
    own_real, own_imag = first[:half], first[half:]
    real, imag = second[:half], second[half:]
    return own_real * real + own_imag * imag, own_imag * real - own_real * imag


def inside_kernel(place_ref, head_ref, list_ref, scale_ref, own_ref, near_ref, out_hbm, border_ref, result, sem, *totals):
    slots, rows = own_ref.shape[0] - 1, own_ref.shape[1]
    half = rows // 2
    offsets = len(totals)
    for total in totals:
        total[...] = jnp.zeros(total.shape, jnp.float32)

    def one_slot(slot, carry):
        pixel = place_ref[OFFSETS + 2, slot]
        column = pixel % totals[0].shape[0]
        own = own_ref[slot]
        for j, total in enumerate(totals):
            real, imag = cross_terms(own, own_ref[jnp.minimum(place_ref[j, pixel], slots)])
            total[column, :half] += real
            total[column, half:] += imag
        return carry

    lax.fori_loop(0, head_ref[0], one_slot, 0)
    for column in range(totals[0].shape[0]):
        for j, total in enumerate(totals):
            at = column * offsets + j
            scaling = scale_ref[j, column]
            result[at, pl.ds(0, half, stride=2), :] = total[column, :half] * scaling
            result[at, pl.ds(1, half, stride=2), :] = total[column, half:] * scaling

    near_row = head_ref[4]

    def one_pair(pair, carry):
        slot, other, at = unpacked(list_ref[near_row, pair])
        real, imag = cross_terms(own_ref[slot], near_ref[other - slots])
        scaling = scale_ref[at % offsets, at // offsets]
        result[at, pl.ds(0, half, stride=2), :] += real * scaling
        result[at, pl.ds(1, half, stride=2), :] += imag * scaling
        return carry

    lax.fori_loop(0, head_ref[1], one_pair, 0)
    copy = pltpu.make_async_copy(result, out_hbm, sem)
    copy.start()
    base = head_ref[2]
    for spot in range(2 * REACH):
        border_ref[spot] = result[base + spot // 2 * offsets + spot % 2]
    copy.wait()


def inside(places, head, near_pairs, scale, own, near, tile_width, offsets):
    rows = own.shape[1]
    spots = tile_width * offsets
    small = pl.BlockSpec(memory_space=pltpu.SMEM)
    whole = pl.BlockSpec(memory_space=pltpu.VMEM)
    return pl.pallas_call(
        inside_kernel,
        name="inside",
        out_shape=(
            pltpu.HBM((spots, rows, LANES), jnp.float32),
            jax.ShapeDtypeStruct((2 * REACH, rows, LANES), jnp.float32),
        ),
        in_specs=[small] * 4 + [whole] * 2,
        out_specs=(pl.BlockSpec(memory_space=pl.ANY), whole),
        scratch_shapes=[pltpu.VMEM((spots, rows, LANES), jnp.float32), pltpu.SemaphoreType.DMA]
        + [pltpu.VMEM((tile_width, rows, LANES), jnp.float32)] * offsets,
        compiler_params=pltpu.CompilerParams(vmem_limit_bytes=16 * 2**20),
        cost_estimate=pl.CostEstimate(flops=60_000_000, bytes_accessed=4_000_000, transcendentals=0),
    )(places, head, near_pairs, scale, own, near)


def across_kernel(head_ref, list_ref, scale_ref, own_ref, far_ref, border_ref, part_hbm, out_hbm, result, sem, *totals):
    del part_hbm
    slots, rows = own_ref.shape[0] - 1, own_ref.shape[1]
    half = rows // 2
    first_far = slots + ROWS * REACH
    offsets = scale_ref.shape[0] // 2
    base = head_ref[2]
    for total in totals:
        total[...] = jnp.zeros(total.shape, jnp.float32)

    far_row = head_ref[5]

    def some_pairs(group, carry):
        for which, total in enumerate(totals):
            slot, other, at = unpacked(list_ref[far_row, group * len(totals) + which])
            spot = (at - base) // offsets * 2 + (at - base) % offsets
            real, imag = cross_terms(own_ref[slot], far_ref[other - first_far])
            total[spot, :half] += real
            total[spot, half:] += imag
        return carry

    pairs = head_ref[3]
    lax.fori_loop(0, (pairs + len(totals) - 1) // len(totals), some_pairs, 0)
    copies = []
    for column in range(REACH):
        for j in range(2):
            spot = 2 * column + j
            at = base + column * offsets + j
            scaling = scale_ref[at % offsets, at // offsets]
            total = totals[0][spot]
            for other in totals[1:]:
                total = total + other[spot]
            total = total * scaling
            result[spot, pl.ds(0, half, stride=2), :] = border_ref[spot, pl.ds(0, half, stride=2), :] + total[:half]
            result[spot, pl.ds(1, half, stride=2), :] = border_ref[spot, pl.ds(1, half, stride=2), :] + total[half:]
        copies.append(
            pltpu.make_async_copy(
                result.at[pl.ds(2 * column, 2)], out_hbm.at[pl.ds(base + column * offsets, 2)], sem.at[column]
            )
        )
        copies[-1].start()
    for copy in copies:
        copy.wait()


def across(head, far_pairs, scale, own, far, border, part):
    rows = own.shape[1]
    small = pl.BlockSpec(memory_space=pltpu.SMEM)
    whole = pl.BlockSpec(memory_space=pltpu.VMEM)
    place = pl.BlockSpec(memory_space=pl.ANY)
    return pl.pallas_call(
        across_kernel,
        name="across",
        out_shape=pltpu.HBM(part.shape, part.dtype),
        in_specs=[small, small, small, whole, whole, whole, place],
        out_specs=place,
        scratch_shapes=[pltpu.VMEM((2 * REACH, rows, LANES), jnp.float32), pltpu.SemaphoreType.DMA((REACH,))]
        + [pltpu.VMEM((2 * REACH, rows, LANES), jnp.float32)] * LANES_OF_PAIRS,
        input_output_aliases={6: 0},
        compiler_params=pltpu.CompilerParams(vmem_limit_bytes=16 * 2**20),
    )(head, far_pairs, scale, own, far, border, part)


def plan_kernel(offset_ref, position_ref, count_ref, map_ref, table_ref, scale_ref, level_ref):
    tile_count, pixels = map_ref.shape
    slots = pixels // 2
    tile_width = pixels // ROWS
    edge = ROWS * REACH
    empty = slots + 2 * edge
    position = position_ref[0]
    offsets = [(offset_ref[j, 0], offset_ref[j, 1]) for j in range(offset_ref.shape[0])]
    held = jnp.where(
        lax.broadcasted_iota(jnp.int32, (tile_count, slots), 1) < count_ref[...], map_ref[:, :slots], -1
    )
    pixel = lax.broadcasted_iota(jnp.int32, (tile_count, pixels), 1)
    tile = lax.broadcasted_iota(jnp.int32, (tile_count, pixels), 0)
    row = pixel // tile_width
    column = pixel % tile_width
    found = jnp.zeros((tile_count, pixels), jnp.int32)
    for slot in range(slots):
        found = jnp.where(held[:, slot : slot + 1] == pixel, slot + 1, found)
    valid = jnp.where(found > 0, 1, 0)
    left_valid = jnp.where(tile > 0, pltpu.roll(valid, 1, 0), 0)
    right_valid = jnp.where(tile < tile_count - 1, pltpu.roll(valid, tile_count - 1, 0), 0)

    def turned(values, shift):
        return pltpu.roll(values, lax.rem(shift + 2 * pixels, pixels), 1)

    for_left = jnp.zeros((tile_count, pixels), jnp.int32)
    for_right = jnp.zeros((tile_count, pixels), jnp.int32)
    for down, across_by in offsets:
        shift = down * tile_width + across_by
        inside_rows = (row >= down) & (row < ROWS + down)
        partner = turned(left_valid, shift - tile_width)
        for_left = jnp.where(inside_rows & (column < across_by), jnp.maximum(for_left, partner), for_left)
        partner = turned(right_valid, shift + tile_width)
        for_right = jnp.where(
            inside_rows & (column >= tile_width + across_by), jnp.maximum(for_right, partner), for_right
        )
    before = jnp.where(
        lax.broadcasted_iota(jnp.int32, (pixels, pixels), 0) <= lax.broadcasted_iota(jnp.int32, (pixels, pixels), 1),
        1.0,
        0.0,
    ).astype(jnp.bfloat16)

    def numbered(needed):
        needed = (needed * valid).astype(jnp.float32)
        ranks = jnp.dot(needed.astype(jnp.bfloat16), before, preferred_element_type=jnp.float32) * needed
        return ranks.astype(jnp.int32), jnp.max(ranks)

    left_rank, left_most = numbered(for_left)
    right_rank, right_most = numbered(for_right)
    most = jnp.maximum(left_most, right_most)
    level_ref[0] = sum([jnp.where(most <= cap, 0, 1) for cap in CAPS])

    def chosen(values, which):
        picked = jnp.sum(jnp.where(tile == which, values, 0), axis=0, keepdims=True)
        return jnp.broadcast_to(picked, (8, pixels))

    odd = lax.rem(position, 2)
    row, column = row[:8], column[:8]
    own = chosen(found, position)
    right = chosen(left_rank, position + 1)
    left = chosen(right_rank, position - 1)
    own_place = jnp.where(own > 0, own - 1, empty)
    right_place = jnp.where(right > 0, slots + odd * edge - 1 + right, empty)
    left_place = jnp.where(left > 0, slots + (1 - odd) * edge - 1 + left, empty)
    selector = jnp.where(
        lax.broadcasted_iota(jnp.int32, (pixels, LANES), 0) % tile_width
        == lax.broadcasted_iota(jnp.int32, (pixels, LANES), 1),
        1.0,
        0.0,
    ).astype(jnp.bfloat16)
    spot = lax.broadcasted_iota(jnp.int32, (8, pixels), 0)
    seen = jnp.zeros((8, pixels), jnp.float32)
    table = jnp.zeros((8, pixels), jnp.int32)
    codes = jnp.where(spot == len(offsets), own - 1, -1)
    for j, (down, across_by) in enumerate(offsets):
        shift = down * tile_width + across_by
        other = turned(own_place, -shift)
        other = jnp.where(column + across_by < 0, turned(left_place, -shift - tile_width), other)
        other = jnp.where(column + across_by >= tile_width, turned(right_place, tile_width - shift), other)
        other = jnp.where((row + down >= 0) & (row + down < ROWS), other, empty)
        seen = jnp.where((spot == j) & (own > 0) & (other < empty), 1.0, seen)
        table = jnp.where(spot == j, other, table)
        code = ((column * len(offsets) + j) * PART + other) * PART + own - 1
        crossing = (spot == j) & (own > 0) & (other >= slots) & (other < empty)
        codes = jnp.where(crossing, code, codes)
    own_left = chosen(left_rank, position)
    own_right = chosen(right_rank, position)
    near = jnp.where(odd == 1, own_left, own_right)
    far = jnp.where(odd == 1, own_right, own_left)
    table = jnp.where(spot == len(offsets), jnp.where(near > 0, near - 1, edge), table)
    table = jnp.where(spot == len(offsets) + 1, jnp.where(far > 0, far - 1, edge), table)
    wide = jnp.concatenate([held, held], axis=1)
    table_ref[:8, :] = jnp.where(spot == len(offsets) + 2, chosen(wide, position), table)
    table_ref[8:, :] = codes
    pairs = jnp.dot(seen.astype(jnp.bfloat16), selector, preferred_element_type=jnp.float32)
    scale_ref[...] = 1.0 / jnp.maximum(pairs, 1.0)


def listing_kernel(table_ref, count_ref, position_ref, head_ref, send_ref, list_ref):
    slots = table_ref.shape[1] // 2
    tile_width = table_ref.shape[1] // ROWS
    edge = ROWS * REACH
    position = position_ref[0]
    odd = lax.rem(position, 2)

    def clear(spot, carry):
        send_ref[spot] = 0
        return carry

    lax.fori_loop(0, 2 * (edge + 1), clear, 0, unroll=26)

    def one_row(row, listed):
        listed = list(listed)
        for side, first_column in enumerate((0, tile_width - REACH)):
            for column in range(first_column, first_column + REACH):
                pixel = row * tile_width + column
                slot = table_ref[8 + OFFSETS, pixel]
                send_ref[table_ref[OFFSETS, pixel]] = slot
                send_ref[edge + 1 + table_ref[OFFSETS + 1, pixel]] = slot
                for j in range(OFFSETS // 2):
                    code = table_ref[8 + (1 - side) * (OFFSETS // 2) + j, pixel]
                    list_ref[side, listed[side]] = code
                    listed[side] = listed[side] + jnp.where(code >= 0, 1, 0)
        return tuple(listed)

    left, right = lax.fori_loop(0, ROWS, one_row, (0, 0))
    base = jnp.where(odd == 1, (tile_width - REACH) * OFFSETS, OFFSETS // 2)
    close = jnp.where(odd == 1, left, right)
    distant = jnp.where(odd == 1, right, left)
    for spare in range(LANES_OF_PAIRS - 1):
        list_ref[odd, distant + spare] = (base * PART + slots + edge) * PART + slots
    count = count_ref[position]
    send_ref[2 * (edge + 1)] = count
    for spot, value in enumerate((count, close, base, distant, 1 - odd, odd)):
        head_ref[spot] = value


def plan(valid_count, block_map, offsets, position):
    tile_count, pixels = block_map.shape
    slots = pixels // 2
    small = pl.BlockSpec(memory_space=pltpu.SMEM)
    whole = pl.BlockSpec(memory_space=pltpu.VMEM)
    position = jnp.full((1,), position, jnp.int32)
    table, scale, level = pl.pallas_call(
        plan_kernel,
        name="plan",
        out_shape=(
            jax.ShapeDtypeStruct((16, pixels), jnp.int32),
            jax.ShapeDtypeStruct((8, LANES), jnp.float32),
            jax.ShapeDtypeStruct((1,), jnp.int32),
        ),
        in_specs=[small, small, whole, whole],
        out_specs=(whole, whole, small),
        compiler_params=pltpu.CompilerParams(vmem_limit_bytes=16 * 2**20),
    )(offsets, position, valid_count.reshape(tile_count, 1), block_map)
    head, send, listed = pl.pallas_call(
        listing_kernel,
        name="listing",
        out_shape=(
            jax.ShapeDtypeStruct((6,), jnp.int32),
            jax.ShapeDtypeStruct((2 * (ROWS * REACH + 1) + 1,), jnp.int32),
            jax.ShapeDtypeStruct((2, ROWS * REACH * OFFSETS // 2 + LANES_OF_PAIRS), jnp.int32),
        ),
        in_specs=[small, small, small],
        out_specs=(small,) * 3,
        compiler_params=pltpu.CompilerParams(vmem_limit_bytes=16 * 2**20),
    )(table, valid_count, position)
    return table, scale, level[0], head, send, listed


def finish(level, near_pairs, far_pairs, tile_width, offsets, operands):
    places, head, scale, listed, own, *edges = operands
    nears, fars = edges[: len(edges) // 2], edges[len(edges) // 2 :]
    if level < len(CAPS):
        near, far = nears[level], fars[level]
    else:
        near, far = jnp.concatenate(nears[-2:]), jnp.concatenate(fars[-2:])
    far = lax.ppermute(far, "tm", far_pairs)
    near = lax.ppermute(near, "tm", near_pairs)
    part, border = inside(places, head, listed, scale, own, near, tile_width, offsets)
    result = across(head, listed, scale, own, far, border, part)
    groups = result.shape[1] // 2
    result = result.reshape(tile_width, offsets, groups, 2, LANES)
    return result.transpose(0, 1, 3, 2, 4).reshape(tile_width, offsets, 2, groups * LANES)


def per_device(frames, frame_valid, valid_count, block_map, offsets):
    devices = lax.axis_size("tm")
    position = lax.axis_index("tm")
    frame_dev = frames.shape[0]
    frames_len = frame_dev * devices
    tile_pix = block_map.shape[1]
    slots = tile_pix // 2
    tile_width = tile_pix // ROWS
    table, twiddle = dft_tables(frames_len)
    per_phase = frame_dev // RADIX
    if devices == PAIRED and per_phase % 16 == 0:
        order = send_order(devices)
        sent = compact_paired(frames, frame_valid, valid_count, block_map)
        pairs = [[(i, i ^ which) for i in range(devices)] for which in order]
        tile_frames = [lax.ppermute(sent[which], "tm", pair) for which, pair in zip(order, pairs)] + [sent[0]]
        table = turn_table(table, position, order + [0])
    else:
        sent = compact(frames, frame_valid, valid_count, block_map)
        received = lax.all_to_all(sent, "tm", split_axis=0, concat_axis=0, tiled=True)
        if per_phase % 16 != 0 or devices == RADIX:
            received = received.reshape(devices, RADIX, per_phase, slots)
            received = received.transpose(1, 0, 2, 3).reshape(RADIX, frames_len // RADIX, slots)
        tile_frames = [received]
    places, scale, level, head, send, listed = plan(valid_count, block_map, offsets, position)
    outs = transform(send, table, twiddle, tile_frames, slots, frames_len)
    far_pairs = [(i, i + 1) for i in range(1, devices - 1, 2)] + [(i + 1, i) for i in range(1, devices - 1, 2)]
    near_pairs = [(i, i + 1) for i in range(0, devices - 1, 2)] + [(i + 1, i) for i in range(0, devices - 1, 2)]
    branches = [
        functools.partial(finish, which, near_pairs, far_pairs, tile_width, offsets.shape[0])
        for which in range(len(CAPS) + 1)
    ]
    return lax.switch(level, branches, (places, head, scale, listed, *outs))


def solution(mesh):
    return jax.shard_map(
        per_device,
        mesh=mesh,
        in_specs=(P("tm", "groups"), P(("groups", "tm")), P("groups"), P("groups", None), P()),
        out_specs=P(("groups", "tm"), None, None, None),
        check_vma=False,
    )
```

```python
import functools
import math

import jax
import jax.numpy as jnp
import numpy as np
from jax import lax
from jax.experimental import pallas as pl
from jax.experimental.pallas import tpu as pltpu
from jax.sharding import PartitionSpec as P

ROWS = 16
REACH = 4
RADIX = 16
LANES = 128
OFFSETS = 4
PART = 512
CAPS = (12, 16, 20, 24, 28, 32)
LANES_OF_PAIRS = 2
PAIRED = 16


def dft_tables(frames_len):
    inner = frames_len // RADIX
    steps = np.arange(inner)
    angles = 2.0 * np.pi * (np.outer(steps, steps) % inner) / inner
    table = np.concatenate([np.cos(angles), -np.sin(angles)], axis=1) / math.sqrt(frames_len)
    turns = 2.0 * np.pi * np.outer(np.arange(RADIX), steps) / frames_len
    twiddle = np.stack([np.cos(turns), -np.sin(turns)], axis=1)
    twiddle = np.broadcast_to(twiddle[:, :, None, :], (RADIX, 2, 8, inner))
    return jnp.asarray(table, jnp.bfloat16), jnp.asarray(twiddle, jnp.float32)


def compact_kernel(count_hbm, valid_hbm, map_hbm, frames_hbm, out_hbm, frames, out_ref, keep, rows, count_ref, valid_ref, map_ref, sems, out_sems, small_sems):
    tile_count, frame_dev, slots = out_ref.shape
    tile_pix = map_ref.shape[1]
    batch = frames.shape[2] // tile_pix
    per_phase = frame_dev // RADIX
    pitch = RADIX + 1
    copies = []
    for step in range(frames.shape[0]):
        span = pl.ds(step * batch * tile_pix, batch * tile_pix)
        copies.append(pltpu.make_async_copy(frames_hbm.at[:, span], frames.at[step], sems.at[step]))
        copies[-1].start()
    smalls = [
        pltpu.make_async_copy(valid_hbm, valid_ref, small_sems.at[0]),
        pltpu.make_async_copy(map_hbm, map_ref, small_sems.at[1]),
        pltpu.make_async_copy(count_hbm, count_ref, small_sems.at[2]),
    ]
    for small in smalls:
        small.start()
    for small in smalls:
        small.wait()
    row = lax.broadcasted_iota(jnp.int32, (frame_dev, frame_dev), 0)
    col = lax.broadcasted_iota(jnp.int32, (frame_dev, frame_dev), 1)
    source = row % per_phase * RADIX + row // per_phase
    usable = jnp.broadcast_to(valid_ref[...], (frame_dev, frame_dev))
    order = jnp.where(col == source, usable, 0).astype(jnp.float32).astype(jnp.bfloat16)
    ones = jnp.ones((frame_dev, slots), jnp.bfloat16)
    keep[...] = jnp.dot(order, ones, preferred_element_type=jnp.float32)
    pixel = lax.broadcasted_iota(jnp.int32, (tile_pix, slots), 0)
    slot = lax.broadcasted_iota(jnp.int32, (1, slots), 1)

    def one_tile(step, which):
        tile = step * batch + which
        held = jnp.where(slot < count_ref[tile], map_ref[tile : tile + 1, :slots], -1)
        hot = jnp.where(jnp.broadcast_to(held, (tile_pix, slots)) == pixel, 1.0, 0.0).astype(jnp.bfloat16)
        block = frames[step, :, which * tile_pix : (which + 1) * tile_pix]
        picked = jnp.dot(block, hot, preferred_element_type=jnp.float32)
        for part in range(per_phase):
            rows[which, pl.ds(part * pitch, RADIX), :] = picked[part * RADIX : (part + 1) * RADIX, :]
        for phase in range(RADIX):
            span = pl.ds(phase * per_phase, per_phase)
            taken = rows[which, pl.ds(phase, per_phase, stride=pitch), :] * keep[span, :]
            out_ref[tile, span, :] = taken.astype(jnp.bfloat16)

    for step, copy in enumerate(copies):
        copy.wait()
        for which in range(batch):
            one_tile(step, which)
        span = pl.ds(step * batch, batch)
        copies[step] = pltpu.make_async_copy(out_ref.at[span], out_hbm.at[span], out_sems.at[step])
        copies[step].start()
    for copy in copies:
        copy.wait()


def compact(frames, frame_valid, valid_count, block_map):
    frame_dev, pixel_count = frames.shape
    tile_count, tile_pix = block_map.shape
    slots = tile_pix // 2
    batch = 4
    steps = tile_count // batch
    place = pl.BlockSpec(memory_space=pl.ANY)
    return pl.pallas_call(
        compact_kernel,
        name="compact",
        out_shape=jax.ShapeDtypeStruct((tile_count, frame_dev, slots), jnp.bfloat16),
        in_specs=[place] * 4,
        out_specs=place,
        scratch_shapes=[
            pltpu.VMEM((steps, frame_dev, batch * tile_pix), jnp.bfloat16),
            pltpu.VMEM((tile_count, frame_dev, slots), jnp.bfloat16),
            pltpu.VMEM((frame_dev, slots), jnp.float32),
            pltpu.VMEM((batch, frame_dev // RADIX * (RADIX + 1) + 7, slots), jnp.float32),
            pltpu.SMEM((tile_count,), jnp.int32),
            pltpu.VMEM((1, frame_dev), jnp.int32),
            pltpu.VMEM((tile_count, tile_pix), jnp.int32),
            pltpu.SemaphoreType.DMA((steps,)),
            pltpu.SemaphoreType.DMA((steps,)),
            pltpu.SemaphoreType.DMA((3,)),
        ],
        compiler_params=pltpu.CompilerParams(vmem_limit_bytes=62 * 2**20),
    )(valid_count, frame_valid.reshape(1, frame_dev), block_map, frames)


def send_order(devices):
    half = devices // 2
    near = list(range(1, half))
    step = half // 2
    far = [half + (i % 2) * step + i // 2 for i in range(half)]
    order = []
    for i, which in enumerate(far):
        order.append(which)
        if i < len(near):
            order.append(near[i])
    return order


def paired_kernel(group, count_hbm, valid_hbm, map_hbm, frames_hbm, *rest):
    *outs, frames, keep, rows, count_ref, valid_ref, map_ref, sems, small_sems = rest
    position = lax.axis_index("tm")
    frame_dev, slots = outs[0].shape
    tile_count, tile_pix = map_ref.shape
    per_phase = frame_dev // RADIX
    pitch = RADIX + 1
    steps = tile_count // group
    steps_order = [(step + steps // 2) % steps for step in range(steps)]
    copies = {}
    for step in steps_order:
        first = jnp.bitwise_xor(position, step * group) // group * group
        span = pl.ds(pl.multiple_of(first * tile_pix, group * tile_pix), group * tile_pix)
        copies[step] = pltpu.make_async_copy(frames_hbm.at[:, span], frames.at[step], sems.at[step])
        copies[step].start()
    smalls = [
        pltpu.make_async_copy(valid_hbm, valid_ref, small_sems.at[0]),
        pltpu.make_async_copy(map_hbm, map_ref, small_sems.at[1]),
        pltpu.make_async_copy(count_hbm, count_ref, small_sems.at[2]),
    ]
    for small in smalls:
        small.start()
    for small in smalls:
        small.wait()
    row = lax.broadcasted_iota(jnp.int32, (frame_dev, frame_dev), 0)
    col = lax.broadcasted_iota(jnp.int32, (frame_dev, frame_dev), 1)
    source = row % per_phase * RADIX + row // per_phase
    usable = jnp.broadcast_to(valid_ref[...], (frame_dev, frame_dev))
    order = jnp.where(col == source, usable, 0).astype(jnp.float32).astype(jnp.bfloat16)
    ones = jnp.ones((frame_dev, slots), jnp.bfloat16)
    keep[...] = jnp.dot(order, ones, preferred_element_type=jnp.float32)
    pixel = lax.broadcasted_iota(jnp.int32, (tile_pix, slots), 0)
    slot = lax.broadcasted_iota(jnp.int32, (1, slots), 1)
    tiles = lax.broadcasted_iota(jnp.int32, (tile_count, slots), 0)
    for step in steps_order:
        copies[step].wait()
        for which in range(group):
            out_ref = outs[step * group + which]
            tile = jnp.bitwise_xor(position, step * group + which)
            held = jnp.sum(jnp.where(tiles == tile, map_ref[:, :slots], 0), axis=0, keepdims=True)
            held = jnp.where(slot < count_ref[tile], held, -1)
            hot = jnp.where(jnp.broadcast_to(held, (tile_pix, slots)) == pixel, 1.0, 0.0).astype(jnp.bfloat16)
            block = frames[step, :, pl.ds(pl.multiple_of(tile % group * tile_pix, tile_pix), tile_pix)]
            picked = jnp.dot(block, hot, preferred_element_type=jnp.float32)
            for part in range(per_phase):
                rows[which, pl.ds(part * pitch, RADIX), :] = picked[part * RADIX : (part + 1) * RADIX, :]
            for phase in range(RADIX):
                span = pl.ds(phase * per_phase, per_phase)
                taken = rows[which, pl.ds(phase, per_phase, stride=pitch), :] * keep[span, :]
                out_ref[span, :] = taken.astype(jnp.bfloat16)


def compact_paired(frames, frame_valid, valid_count, block_map):
    frame_dev, pixel_count = frames.shape
    tile_count, tile_pix = block_map.shape
    slots = tile_pix // 2
    group = 4
    steps = tile_count // group
    place = pl.BlockSpec(memory_space=pl.ANY)
    return pl.pallas_call(
        functools.partial(paired_kernel, group),
        name="compact",
        out_shape=[jax.ShapeDtypeStruct((frame_dev, slots), jnp.bfloat16)] * tile_count,
        in_specs=[place] * 4,
        out_specs=[pl.BlockSpec(memory_space=pltpu.VMEM)] * tile_count,
        scratch_shapes=[
            pltpu.VMEM((steps, frame_dev, group * tile_pix), jnp.bfloat16),
            pltpu.VMEM((frame_dev, slots), jnp.float32),
            pltpu.VMEM((group, frame_dev // RADIX * (RADIX + 1) + 7, slots), jnp.float32),
            pltpu.SMEM((tile_count,), jnp.int32),
            pltpu.VMEM((1, frame_dev), jnp.int32),
            pltpu.VMEM((tile_count, tile_pix), jnp.int32),
            pltpu.SemaphoreType.DMA((steps,)),
            pltpu.SemaphoreType.DMA((3,)),
        ],
        compiler_params=pltpu.CompilerParams(vmem_limit_bytes=16 * 2**20),
    )(
        pltpu.with_memory_space_constraint(valid_count, pltpu.HBM),
        pltpu.with_memory_space_constraint(frame_valid.reshape(1, frame_dev), pltpu.HBM),
        pltpu.with_memory_space_constraint(block_map, pltpu.HBM),
        pltpu.with_memory_space_constraint(frames, pltpu.HBM),
    )


def turn_kernel(order, position_ref, table_ref, out_ref):
    per_phase = table_ref.shape[0] // len(order)
    for place, which in enumerate(order):
        source = jnp.bitwise_xor(position_ref[0], which)
        rows = pl.ds(pl.multiple_of(source * per_phase, per_phase), per_phase)
        out_ref[pl.ds(place * per_phase, per_phase), :] = table_ref[rows, :]


def turn_table(table, position, order):
    whole = pl.BlockSpec(memory_space=pltpu.VMEM)
    return pl.pallas_call(
        functools.partial(turn_kernel, order),
        name="turn",
        out_shape=jax.ShapeDtypeStruct(table.shape, table.dtype),
        in_specs=[pl.BlockSpec(memory_space=pltpu.SMEM), whole],
        out_specs=whole,
        compiler_params=pltpu.CompilerParams(vmem_limit_bytes=16 * 2**20),
    )(jnp.full((1,), position, jnp.int32), table)


def rotate(real, imag, cos, sin):
    return real * cos - imag * sin, real * sin + imag * cos


def four_point(values):
    (r0, i0), (r1, i1), (r2, i2), (r3, i3) = values
    er, ei, fr, fi = r0 + r2, i0 + i2, r0 - r2, i0 - i2
    gr, gi, hr, hi = r1 + r3, i1 + i3, r1 - r3, i1 - i3
    return [(er + gr, ei + gi), (fr + hi, fi - hr), (er - gr, ei - gi), (fr - hi, fi + hr)]


def sixteen_point_low(values):
    inner = [four_point([values[4 * n + m] for n in range(4)]) for m in range(4)]
    low = [None] * 8
    for k in range(4):
        parts = []
        for m in range(4):
            real, imag = inner[m][k]
            turn = m * k % 16
            if turn == 0:
                parts.append((real, imag))
            elif turn == 4:
                parts.append((imag, -real))
            else:
                angle = -2.0 * math.pi * turn / 16
                parts.append(rotate(real, imag, math.cos(angle), math.sin(angle)))
        (r0, i0), (r1, i1), (r2, i2), (r3, i3) = parts
        low[k] = ((r0 + r2) + (r1 + r3), (i0 + i2) + (i1 + i3))
        low[k + 4] = ((r0 - r2) + (i1 - i3), (i0 - i2) - (r1 - r3))
    return low


def transform_kernel(blocks, send_ref, table_ref, twiddle_ref, *rest):
    frames, own_ref = rest[:blocks], rest[blocks]
    edges, (phases, spread) = rest[blocks + 1 : -2], rest[-2:]
    slots = own_ref.shape[0] - 1
    rows = own_ref.shape[1]
    pitch = rows + 1
    half = rows // 2
    inner = table_ref.shape[0]
    edge = ROWS * REACH
    for phase in range(RADIX):
        if blocks > 1:
            per_phase = inner // blocks
            span = slice(phase * per_phase, (phase + 1) * per_phase)
            block = jnp.concatenate([ref[span, :] for ref in frames], axis=0)
        elif frames[0].shape[0] != RADIX:
            per_phase = frames[0].shape[1] // RADIX
            block = frames[0][:, phase * per_phase : (phase + 1) * per_phase, :].reshape(inner, slots)
        else:
            block = frames[0][phase].reshape(inner, slots)
        phases[phase] = lax.dot_general(
            block, table_ref[...], (((0,), (0,)), ((), ())), preferred_element_type=jnp.float32
        )
    groups = (send_ref[2 * (edge + 1)] + 7) // 8
    chunks = inner // LANES

    def one_group(group, carry):
        first = pl.multiple_of(group * 8, 8)
        for chunk in range(chunks):
            lanes = pl.ds(chunk * LANES, LANES)
            values = []
            for phase in range(RADIX):
                real = phases[phase, pl.ds(first, 8), lanes]
                imag = phases[phase, pl.ds(first, 8), pl.ds(inner + chunk * LANES, LANES)]
                if phase > 0:
                    real, imag = rotate(real, imag, twiddle_ref[phase, 0, :, lanes], twiddle_ref[phase, 1, :, lanes])
                values.append((real, imag))
            for high, (real, imag) in enumerate(sixteen_point_low(values)):
                at = first * pitch + high * chunks + chunk
                spread[pl.ds(at, 8, stride=pitch), :] = real
                spread[pl.ds(at + half, 8, stride=pitch), :] = imag
        return carry

    lax.fori_loop(0, groups, one_group, 0)

    def eight_slots(group, carry):
        for slot in range(8):
            slot = group * 8 + slot
            own_ref[slot] = spread[pl.ds(slot * pitch, rows), :].astype(jnp.bfloat16)
        return carry

    lax.fori_loop(0, groups, eight_slots, 0)
    own_ref[slots] = jnp.zeros((rows, LANES), jnp.bfloat16)
    nears, fars = edges[:2], edges[2:]
    bounds = [0] + [ref.shape[0] for ref in fars[:-1]]
    for low, high in zip(bounds[:-1], bounds[1:]):

        def one_edge(spot, carry, high=high):
            nears[0][spot] = own_ref[send_ref[spot]]
            block = own_ref[send_ref[edge + 1 + spot]]
            for ref in fars[:-1]:
                if ref.shape[0] >= high:
                    ref[spot] = block
            return carry

        lax.fori_loop(low, high, one_edge, 0, unroll=4)

    def one_rest(spot, carry):
        nears[1][spot] = own_ref[send_ref[bounds[-1] + spot]]
        fars[-1][spot] = own_ref[send_ref[edge + 1 + bounds[-1] + spot]]
        return carry

    lax.fori_loop(0, edge - bounds[-1], one_rest, 0, unroll=4)


def transform(send, table, twiddle, tile_frames, slots, frames_len):
    inner = frames_len // RADIX
    rows = frames_len // LANES
    edge = ROWS * REACH
    sizes = [CAPS[-1], edge - CAPS[-1], *CAPS, edge - CAPS[-1]]
    whole = pl.BlockSpec(memory_space=pltpu.VMEM)
    return pl.pallas_call(
        functools.partial(transform_kernel, len(tile_frames)),
        name="transform",
        out_shape=(
            jax.ShapeDtypeStruct((slots + 1, rows, LANES), jnp.bfloat16),
            *[jax.ShapeDtypeStruct((size, rows, LANES), jnp.bfloat16) for size in sizes],
        ),
        in_specs=[pl.BlockSpec(memory_space=pltpu.SMEM)] + [whole] * (2 + len(tile_frames)),
        out_specs=(whole,) * (1 + len(sizes)),
        scratch_shapes=[
            pltpu.VMEM((RADIX, slots, 2 * inner), jnp.float32),
            pltpu.VMEM((slots * (rows + 1) + 7, LANES), jnp.float32),
        ],
        compiler_params=pltpu.CompilerParams(vmem_limit_bytes=24 * 2**20),
    )(send, table, twiddle, *tile_frames)


def unpacked(code):
    return code % PART, code // PART % PART, code // PART // PART


def cross_terms(first, second):
    half = first.shape[0] // 2
    first = first.astype(jnp.float32)
    second = second.astype(jnp.float32)
    own_real, own_imag = first[:half], first[half:]
    real, imag = second[:half], second[half:]
    return own_real * real + own_imag * imag, own_imag * real - own_real * imag


def inside_kernel(place_ref, head_ref, list_ref, scale_ref, own_ref, near_ref, result, *totals):
    slots, rows = own_ref.shape[0] - 1, own_ref.shape[1]
    half = rows // 2
    offsets = len(totals)
    for total in totals:
        total[...] = jnp.zeros(total.shape, jnp.float32)

    def one_slot(slot, carry):
        pixel = place_ref[OFFSETS + 2, slot]
        column = pixel % totals[0].shape[0]
        own = own_ref[slot]
        for j, total in enumerate(totals):
            real, imag = cross_terms(own, own_ref[jnp.minimum(place_ref[j, pixel], slots)])
            total[column, :half] += real
            total[column, half:] += imag
        return carry

    lax.fori_loop(0, head_ref[0], one_slot, 0)
    for column in range(totals[0].shape[0]):
        for j, total in enumerate(totals):
            at = column * offsets + j
            scaling = scale_ref[j, column]
            result[at, pl.ds(0, half, stride=2), :] = total[column, :half] * scaling
            result[at, pl.ds(1, half, stride=2), :] = total[column, half:] * scaling

    near_row = head_ref[4]

    def one_pair(pair, carry):
        slot, other, at = unpacked(list_ref[near_row, pair])
        real, imag = cross_terms(own_ref[slot], near_ref[other - slots])
        scaling = scale_ref[at % offsets, at // offsets]
        result[at, pl.ds(0, half, stride=2), :] += real * scaling
        result[at, pl.ds(1, half, stride=2), :] += imag * scaling
        return carry

    lax.fori_loop(0, head_ref[1], one_pair, 0)


def inside(places, head, near_pairs, scale, own, near, tile_width, offsets):
    rows = own.shape[1]
    small = pl.BlockSpec(memory_space=pltpu.SMEM)
    whole = pl.BlockSpec(memory_space=pltpu.VMEM)
    return pl.pallas_call(
        inside_kernel,
        name="inside",
        out_shape=jax.ShapeDtypeStruct((tile_width * offsets, rows, LANES), jnp.float32),
        in_specs=[small] * 4 + [whole] * 2,
        out_specs=whole,
        scratch_shapes=[pltpu.VMEM((tile_width, rows, LANES), jnp.float32)] * offsets,
        compiler_params=pltpu.CompilerParams(vmem_limit_bytes=16 * 2**20),
        cost_estimate=pl.CostEstimate(flops=60_000_000, bytes_accessed=4_000_000, transcendentals=0),
    )(places, head, near_pairs, scale, own, near)


def across_kernel(head_ref, list_ref, scale_ref, own_ref, far_ref, part_ref, out_hbm, result, sem, inner_sem, *totals):
    slots, rows = own_ref.shape[0] - 1, own_ref.shape[1]
    half = rows // 2
    first_far = slots + ROWS * REACH
    spots = part_ref.shape[0]
    offsets = scale_ref.shape[0] // 2
    base = head_ref[2]
    border = REACH * offsets
    odd = head_ref[5]
    safe = pl.ds(jnp.where(odd == 1, 0, border), spots - border)
    inner = pltpu.make_async_copy(part_ref.at[safe], out_hbm.at[safe], inner_sem.at[0])
    inner.start()
    others = []
    for column in range(REACH):
        kept = pl.ds(base + column * offsets + jnp.where(odd == 1, 2, -2), 2)
        others.append(pltpu.make_async_copy(part_ref.at[kept], out_hbm.at[kept], inner_sem.at[1 + column]))
        others[-1].start()
    for total in totals:
        total[...] = jnp.zeros(total.shape, jnp.float32)
    far_row = head_ref[5]

    def some_pairs(group, carry):
        for which, total in enumerate(totals):
            slot, other, at = unpacked(list_ref[far_row, group * len(totals) + which])
            spot = (at - base) // offsets * 2 + (at - base) % offsets
            real, imag = cross_terms(own_ref[slot], far_ref[other - first_far])
            total[spot, :half] += real
            total[spot, half:] += imag
        return carry

    pairs = head_ref[3]
    lax.fori_loop(0, (pairs + len(totals) - 1) // len(totals), some_pairs, 0)
    copies = []
    for column in range(REACH):
        for j in range(2):
            spot = 2 * column + j
            at = base + column * offsets + j
            scaling = scale_ref[at % offsets, at // offsets]
            total = totals[0][spot]
            for other in totals[1:]:
                total = total + other[spot]
            total = total * scaling
            result[spot, pl.ds(0, half, stride=2), :] = part_ref[at, pl.ds(0, half, stride=2), :] + total[:half]
            result[spot, pl.ds(1, half, stride=2), :] = part_ref[at, pl.ds(1, half, stride=2), :] + total[half:]
        copies.append(
            pltpu.make_async_copy(
                result.at[pl.ds(2 * column, 2)], out_hbm.at[pl.ds(base + column * offsets, 2)], sem.at[column]
            )
        )
        copies[-1].start()
    for copy in [inner, *others, *copies]:
        copy.wait()


def across(head, far_pairs, scale, own, far, part):
    rows = own.shape[1]
    small = pl.BlockSpec(memory_space=pltpu.SMEM)
    whole = pl.BlockSpec(memory_space=pltpu.VMEM)
    return pl.pallas_call(
        across_kernel,
        name="across",
        out_shape=pltpu.HBM(part.shape, part.dtype),
        in_specs=[small, small, small, whole, whole, whole],
        out_specs=pl.BlockSpec(memory_space=pl.ANY),
        scratch_shapes=[
            pltpu.VMEM((2 * REACH, rows, LANES), jnp.float32),
            pltpu.SemaphoreType.DMA((REACH,)),
            pltpu.SemaphoreType.DMA((1 + REACH,)),
        ]
        + [pltpu.VMEM((2 * REACH, rows, LANES), jnp.float32)] * LANES_OF_PAIRS,
        compiler_params=pltpu.CompilerParams(vmem_limit_bytes=16 * 2**20),
    )(head, far_pairs, scale, own, far, part)


def plan_kernel(offset_ref, position_ref, count_ref, map_ref, table_ref, scale_ref, level_ref):
    tile_count, pixels = map_ref.shape
    slots = pixels // 2
    tile_width = pixels // ROWS
    edge = ROWS * REACH
    empty = slots + 2 * edge
    position = position_ref[0]
    offsets = [(offset_ref[j, 0], offset_ref[j, 1]) for j in range(offset_ref.shape[0])]
    held = jnp.where(
        lax.broadcasted_iota(jnp.int32, (tile_count, slots), 1) < count_ref[...], map_ref[:, :slots], -1
    )
    pixel = lax.broadcasted_iota(jnp.int32, (tile_count, pixels), 1)
    tile = lax.broadcasted_iota(jnp.int32, (tile_count, pixels), 0)
    row = pixel // tile_width
    column = pixel % tile_width
    found = jnp.zeros((tile_count, pixels), jnp.int32)
    for slot in range(slots):
        found = jnp.where(held[:, slot : slot + 1] == pixel, slot + 1, found)
    valid = jnp.where(found > 0, 1, 0)
    left_valid = jnp.where(tile > 0, pltpu.roll(valid, 1, 0), 0)
    right_valid = jnp.where(tile < tile_count - 1, pltpu.roll(valid, tile_count - 1, 0), 0)

    def turned(values, shift):
        return pltpu.roll(values, lax.rem(shift + 2 * pixels, pixels), 1)

    for_left = jnp.zeros((tile_count, pixels), jnp.int32)
    for_right = jnp.zeros((tile_count, pixels), jnp.int32)
    for down, across_by in offsets:
        shift = down * tile_width + across_by
        inside_rows = (row >= down) & (row < ROWS + down)
        partner = turned(left_valid, shift - tile_width)
        for_left = jnp.where(inside_rows & (column < across_by), jnp.maximum(for_left, partner), for_left)
        partner = turned(right_valid, shift + tile_width)
        for_right = jnp.where(
            inside_rows & (column >= tile_width + across_by), jnp.maximum(for_right, partner), for_right
        )
    before = jnp.where(
        lax.broadcasted_iota(jnp.int32, (pixels, pixels), 0) <= lax.broadcasted_iota(jnp.int32, (pixels, pixels), 1),
        1.0,
        0.0,
    ).astype(jnp.bfloat16)

    def numbered(needed):
        needed = (needed * valid).astype(jnp.float32)
        ranks = jnp.dot(needed.astype(jnp.bfloat16), before, preferred_element_type=jnp.float32) * needed
        return ranks.astype(jnp.int32), jnp.max(ranks)

    left_rank, left_most = numbered(for_left)
    right_rank, right_most = numbered(for_right)
    most = jnp.maximum(left_most, right_most)
    sent_far = jnp.max(jnp.where(tile % 2 == 0, left_rank, right_rank).astype(jnp.float32))
    level = sum([jnp.where(sent_far <= cap, 0, 1) for cap in CAPS])
    level_ref[0] = jnp.where(most <= CAPS[-1], level, len(CAPS))

    def chosen(values, which):
        picked = jnp.sum(jnp.where(tile == which, values, 0), axis=0, keepdims=True)
        return jnp.broadcast_to(picked, (8, pixels))

    odd = lax.rem(position, 2)
    row, column = row[:8], column[:8]
    own = chosen(found, position)
    right = chosen(left_rank, position + 1)
    left = chosen(right_rank, position - 1)
    own_place = jnp.where(own > 0, own - 1, empty)
    right_place = jnp.where(right > 0, slots + odd * edge - 1 + right, empty)
    left_place = jnp.where(left > 0, slots + (1 - odd) * edge - 1 + left, empty)
    selector = jnp.where(
        lax.broadcasted_iota(jnp.int32, (pixels, LANES), 0) % tile_width
        == lax.broadcasted_iota(jnp.int32, (pixels, LANES), 1),
        1.0,
        0.0,
    ).astype(jnp.bfloat16)
    spot = lax.broadcasted_iota(jnp.int32, (8, pixels), 0)
    seen = jnp.zeros((8, pixels), jnp.float32)
    table = jnp.zeros((8, pixels), jnp.int32)
    codes = jnp.where(spot == len(offsets), own - 1, -1)
    for j, (down, across_by) in enumerate(offsets):
        shift = down * tile_width + across_by
        other = turned(own_place, -shift)
        other = jnp.where(column + across_by < 0, turned(left_place, -shift - tile_width), other)
        other = jnp.where(column + across_by >= tile_width, turned(right_place, tile_width - shift), other)
        other = jnp.where((row + down >= 0) & (row + down < ROWS), other, empty)
        seen = jnp.where((spot == j) & (own > 0) & (other < empty), 1.0, seen)
        table = jnp.where(spot == j, other, table)
        code = ((column * len(offsets) + j) * PART + other) * PART + own - 1
        crossing = (spot == j) & (own > 0) & (other >= slots) & (other < empty)
        codes = jnp.where(crossing, code, codes)
    own_left = chosen(left_rank, position)
    own_right = chosen(right_rank, position)
    near = jnp.where(odd == 1, own_left, own_right)
    far = jnp.where(odd == 1, own_right, own_left)
    table = jnp.where(spot == len(offsets), jnp.where(near > 0, near - 1, edge), table)
    table = jnp.where(spot == len(offsets) + 1, jnp.where(far > 0, far - 1, edge), table)
    wide = jnp.concatenate([held, held], axis=1)
    table_ref[:8, :] = jnp.where(spot == len(offsets) + 2, chosen(wide, position), table)
    table_ref[8:, :] = codes
    pairs = jnp.dot(seen.astype(jnp.bfloat16), selector, preferred_element_type=jnp.float32)
    scale_ref[...] = 1.0 / jnp.maximum(pairs, 1.0)


def listing_kernel(table_ref, count_ref, position_ref, head_ref, send_ref, list_ref):
    slots = table_ref.shape[1] // 2
    tile_width = table_ref.shape[1] // ROWS
    edge = ROWS * REACH
    position = position_ref[0]
    odd = lax.rem(position, 2)

    def clear(spot, carry):
        send_ref[spot] = 0
        return carry

    lax.fori_loop(0, 2 * (edge + 1), clear, 0, unroll=26)

    def one_row(row, listed):
        listed = list(listed)
        for side, first_column in enumerate((0, tile_width - REACH)):
            for column in range(first_column, first_column + REACH):
                pixel = row * tile_width + column
                slot = table_ref[8 + OFFSETS, pixel]
                send_ref[table_ref[OFFSETS, pixel]] = slot
                send_ref[edge + 1 + table_ref[OFFSETS + 1, pixel]] = slot
                for j in range(OFFSETS // 2):
                    code = table_ref[8 + (1 - side) * (OFFSETS // 2) + j, pixel]
                    list_ref[side, listed[side]] = code
                    listed[side] = listed[side] + jnp.where(code >= 0, 1, 0)
        return tuple(listed)

    left, right = lax.fori_loop(0, ROWS, one_row, (0, 0))
    base = jnp.where(odd == 1, (tile_width - REACH) * OFFSETS, OFFSETS // 2)
    close = jnp.where(odd == 1, left, right)
    distant = jnp.where(odd == 1, right, left)
    for spare in range(LANES_OF_PAIRS - 1):
        list_ref[odd, distant + spare] = (base * PART + slots + edge) * PART + slots
    count = count_ref[position]
    send_ref[2 * (edge + 1)] = count
    for spot, value in enumerate((count, close, base, distant, 1 - odd, odd)):
        head_ref[spot] = value


def plan(valid_count, block_map, offsets, position):
    tile_count, pixels = block_map.shape
    slots = pixels // 2
    small = pl.BlockSpec(memory_space=pltpu.SMEM)
    whole = pl.BlockSpec(memory_space=pltpu.VMEM)
    position = jnp.full((1,), position, jnp.int32)
    table, scale, level = pl.pallas_call(
        plan_kernel,
        name="plan",
        out_shape=(
            jax.ShapeDtypeStruct((16, pixels), jnp.int32),
            jax.ShapeDtypeStruct((8, LANES), jnp.float32),
            jax.ShapeDtypeStruct((1,), jnp.int32),
        ),
        in_specs=[small, small, whole, whole],
        out_specs=(whole, whole, small),
        compiler_params=pltpu.CompilerParams(vmem_limit_bytes=16 * 2**20),
    )(offsets, position, valid_count.reshape(tile_count, 1), block_map)
    head, send, listed = pl.pallas_call(
        listing_kernel,
        name="listing",
        out_shape=(
            jax.ShapeDtypeStruct((6,), jnp.int32),
            jax.ShapeDtypeStruct((2 * (ROWS * REACH + 1) + 1,), jnp.int32),
            jax.ShapeDtypeStruct((2, ROWS * REACH * OFFSETS // 2 + LANES_OF_PAIRS), jnp.int32),
        ),
        in_specs=[small, small, small],
        out_specs=(small,) * 3,
        compiler_params=pltpu.CompilerParams(vmem_limit_bytes=16 * 2**20),
    )(table, valid_count, position)
    return table, scale, level[0], head, send, listed


def finish(level, near_pairs, far_pairs, tile_width, offsets, operands):
    places, head, scale, listed, own, *edges = operands
    nears, fars = edges[:2], edges[2:]
    if level < len(CAPS):
        near, far = nears[0], fars[level]
    else:
        near, far = jnp.concatenate(nears), jnp.concatenate(fars[-2:])
    far = lax.ppermute(far, "tm", far_pairs)
    near = lax.ppermute(near, "tm", near_pairs)
    part = inside(places, head, listed, scale, own, near, tile_width, offsets)
    result = across(head, listed, scale, own, far, part)
    groups = result.shape[1] // 2
    result = result.reshape(tile_width, offsets, groups, 2, LANES)
    return result.transpose(0, 1, 3, 2, 4).reshape(tile_width, offsets, 2, groups * LANES)


def per_device(frames, frame_valid, valid_count, block_map, offsets):
    devices = lax.axis_size("tm")
    position = lax.axis_index("tm")
    frame_dev = frames.shape[0]
    frames_len = frame_dev * devices
    tile_pix = block_map.shape[1]
    slots = tile_pix // 2
    tile_width = tile_pix // ROWS
    table, twiddle = dft_tables(frames_len)
    per_phase = frame_dev // RADIX
    if devices == PAIRED and per_phase % 16 == 0:
        order = send_order(devices)
        sent = compact_paired(frames, frame_valid, valid_count, block_map)
        pairs = [[(i, i ^ which) for i in range(devices)] for which in order]
        tile_frames = [lax.ppermute(sent[which], "tm", pair) for which, pair in zip(order, pairs)] + [sent[0]]
        table = turn_table(table, position, order + [0])
    else:
        sent = compact(frames, frame_valid, valid_count, block_map)
        received = lax.all_to_all(sent, "tm", split_axis=0, concat_axis=0, tiled=True)
        if per_phase % 16 != 0 or devices == RADIX:
            received = received.reshape(devices, RADIX, per_phase, slots)
            received = received.transpose(1, 0, 2, 3).reshape(RADIX, frames_len // RADIX, slots)
        tile_frames = [received]
    places, scale, level, head, send, listed = plan(valid_count, block_map, offsets, position)
    outs = transform(send, table, twiddle, tile_frames, slots, frames_len)
    far_pairs = [(i, i + 1) for i in range(1, devices - 1, 2)] + [(i + 1, i) for i in range(1, devices - 1, 2)]
    near_pairs = [(i, i + 1) for i in range(0, devices - 1, 2)] + [(i + 1, i) for i in range(0, devices - 1, 2)]
    branches = [
        functools.partial(finish, which, near_pairs, far_pairs, tile_width, offsets.shape[0])
        for which in range(len(CAPS) + 1)
    ]
    return lax.switch(level, branches, (places, head, scale, listed, *outs))


def solution(mesh):
    return jax.shard_map(
        per_device,
        mesh=mesh,
        in_specs=(P("tm", "groups"), P(("groups", "tm")), P("groups"), P("groups", None), P()),
        out_specs=P(("groups", "tm"), None, None, None),
        check_vma=False,
    )
```

```python
import functools
import math

import jax
import jax.numpy as jnp
import numpy as np
from jax import lax
from jax.experimental import pallas as pl
from jax.experimental.pallas import tpu as pltpu
from jax.sharding import PartitionSpec as P

ROWS = 16
REACH = 4
RADIX = 16
LANES = 128
OFFSETS = 4
PART = 512
CAPS = (12, 16, 20, 24, 28, 32)
LANES_OF_PAIRS = 4
PAIRED = 16


def dft_tables(frames_len):
    inner = frames_len // RADIX
    steps = np.arange(inner)
    angles = 2.0 * np.pi * (np.outer(steps, steps) % inner) / inner
    table = np.concatenate([np.cos(angles), -np.sin(angles)], axis=1) / math.sqrt(frames_len)
    turns = 2.0 * np.pi * np.outer(np.arange(RADIX), steps) / frames_len
    twiddle = np.stack([np.cos(turns), -np.sin(turns)], axis=1)
    twiddle = np.broadcast_to(twiddle[:, :, None, :], (RADIX, 2, 8, inner))
    return jnp.asarray(table, jnp.bfloat16), jnp.asarray(twiddle, jnp.float32)


def compact_kernel(count_hbm, valid_hbm, map_hbm, frames_hbm, out_hbm, frames, out_ref, keep, rows, count_ref, valid_ref, map_ref, sems, out_sems, small_sems):
    tile_count, frame_dev, slots = out_ref.shape
    tile_pix = map_ref.shape[1]
    batch = frames.shape[2] // tile_pix
    per_phase = frame_dev // RADIX
    pitch = RADIX + 1
    copies = []
    for step in range(frames.shape[0]):
        span = pl.ds(step * batch * tile_pix, batch * tile_pix)
        copies.append(pltpu.make_async_copy(frames_hbm.at[:, span], frames.at[step], sems.at[step]))
        copies[-1].start()
    smalls = [
        pltpu.make_async_copy(valid_hbm, valid_ref, small_sems.at[0]),
        pltpu.make_async_copy(map_hbm, map_ref, small_sems.at[1]),
        pltpu.make_async_copy(count_hbm, count_ref, small_sems.at[2]),
    ]
    for small in smalls:
        small.start()
    for small in smalls:
        small.wait()
    row = lax.broadcasted_iota(jnp.int32, (frame_dev, frame_dev), 0)
    col = lax.broadcasted_iota(jnp.int32, (frame_dev, frame_dev), 1)
    source = row % per_phase * RADIX + row // per_phase
    usable = jnp.broadcast_to(valid_ref[...], (frame_dev, frame_dev))
    order = jnp.where(col == source, usable, 0).astype(jnp.float32).astype(jnp.bfloat16)
    ones = jnp.ones((frame_dev, slots), jnp.bfloat16)
    keep[...] = jnp.dot(order, ones, preferred_element_type=jnp.float32)
    pixel = lax.broadcasted_iota(jnp.int32, (tile_pix, slots), 0)
    slot = lax.broadcasted_iota(jnp.int32, (1, slots), 1)

    def one_tile(step, which):
        tile = step * batch + which
        held = jnp.where(slot < count_ref[tile], map_ref[tile : tile + 1, :slots], -1)
        hot = jnp.where(jnp.broadcast_to(held, (tile_pix, slots)) == pixel, 1.0, 0.0).astype(jnp.bfloat16)
        block = frames[step, :, which * tile_pix : (which + 1) * tile_pix]
        picked = jnp.dot(block, hot, preferred_element_type=jnp.float32)
        for part in range(per_phase):
            rows[which, pl.ds(part * pitch, RADIX), :] = picked[part * RADIX : (part + 1) * RADIX, :]
        for phase in range(RADIX):
            span = pl.ds(phase * per_phase, per_phase)
            taken = rows[which, pl.ds(phase, per_phase, stride=pitch), :] * keep[span, :]
            out_ref[tile, span, :] = taken.astype(jnp.bfloat16)

    for step, copy in enumerate(copies):
        copy.wait()
        for which in range(batch):
            one_tile(step, which)
        span = pl.ds(step * batch, batch)
        copies[step] = pltpu.make_async_copy(out_ref.at[span], out_hbm.at[span], out_sems.at[step])
        copies[step].start()
    for copy in copies:
        copy.wait()


def compact(frames, frame_valid, valid_count, block_map):
    frame_dev, pixel_count = frames.shape
    tile_count, tile_pix = block_map.shape
    slots = tile_pix // 2
    batch = 4
    steps = tile_count // batch
    place = pl.BlockSpec(memory_space=pl.ANY)
    return pl.pallas_call(
        compact_kernel,
        name="compact",
        out_shape=jax.ShapeDtypeStruct((tile_count, frame_dev, slots), jnp.bfloat16),
        in_specs=[place] * 4,
        out_specs=place,
        scratch_shapes=[
            pltpu.VMEM((steps, frame_dev, batch * tile_pix), jnp.bfloat16),
            pltpu.VMEM((tile_count, frame_dev, slots), jnp.bfloat16),
            pltpu.VMEM((frame_dev, slots), jnp.float32),
            pltpu.VMEM((batch, frame_dev // RADIX * (RADIX + 1) + 7, slots), jnp.float32),
            pltpu.SMEM((tile_count,), jnp.int32),
            pltpu.VMEM((1, frame_dev), jnp.int32),
            pltpu.VMEM((tile_count, tile_pix), jnp.int32),
            pltpu.SemaphoreType.DMA((steps,)),
            pltpu.SemaphoreType.DMA((steps,)),
            pltpu.SemaphoreType.DMA((3,)),
        ],
        compiler_params=pltpu.CompilerParams(vmem_limit_bytes=62 * 2**20),
    )(valid_count, frame_valid.reshape(1, frame_dev), block_map, frames)


def send_order(devices):
    half = devices // 2
    near = list(range(1, half))
    step = half // 2
    far = [half + (i % 2) * step + i // 2 for i in range(half)]
    order = []
    for i, which in enumerate(far):
        order.append(which)
        if i < len(near):
            order.append(near[i])
    return order


def paired_kernel(group, count_hbm, valid_hbm, map_hbm, frames_hbm, *rest):
    *outs, frames, keep, rows, count_ref, valid_ref, map_ref, sems, small_sems = rest
    position = lax.axis_index("tm")
    frame_dev, slots = outs[0].shape
    tile_count, tile_pix = map_ref.shape
    per_phase = frame_dev // RADIX
    pitch = RADIX + 1
    steps = tile_count // group
    steps_order = [(step + steps // 2) % steps for step in range(steps)]
    copies = {}
    for step in steps_order:
        first = jnp.bitwise_xor(position, step * group) // group * group
        span = pl.ds(pl.multiple_of(first * tile_pix, group * tile_pix), group * tile_pix)
        copies[step] = pltpu.make_async_copy(frames_hbm.at[:, span], frames.at[step], sems.at[step])
        copies[step].start()
    smalls = [
        pltpu.make_async_copy(valid_hbm, valid_ref, small_sems.at[0]),
        pltpu.make_async_copy(map_hbm, map_ref, small_sems.at[1]),
        pltpu.make_async_copy(count_hbm, count_ref, small_sems.at[2]),
    ]
    for small in smalls:
        small.start()
    for small in smalls:
        small.wait()
    row = lax.broadcasted_iota(jnp.int32, (frame_dev, frame_dev), 0)
    col = lax.broadcasted_iota(jnp.int32, (frame_dev, frame_dev), 1)
    source = row % per_phase * RADIX + row // per_phase
    usable = jnp.broadcast_to(valid_ref[...], (frame_dev, frame_dev))
    order = jnp.where(col == source, usable, 0).astype(jnp.float32).astype(jnp.bfloat16)
    ones = jnp.ones((frame_dev, slots), jnp.bfloat16)
    keep[...] = jnp.dot(order, ones, preferred_element_type=jnp.float32)
    pixel = lax.broadcasted_iota(jnp.int32, (tile_pix, slots), 0)
    slot = lax.broadcasted_iota(jnp.int32, (1, slots), 1)
    tiles = lax.broadcasted_iota(jnp.int32, (tile_count, slots), 0)
    for step in steps_order:
        copies[step].wait()
        for which in range(group):
            out_ref = outs[step * group + which]
            tile = jnp.bitwise_xor(position, step * group + which)
            held = jnp.sum(jnp.where(tiles == tile, map_ref[:, :slots], 0), axis=0, keepdims=True)
            held = jnp.where(slot < count_ref[tile], held, -1)
            hot = jnp.where(jnp.broadcast_to(held, (tile_pix, slots)) == pixel, 1.0, 0.0).astype(jnp.bfloat16)
            block = frames[step, :, pl.ds(pl.multiple_of(tile % group * tile_pix, tile_pix), tile_pix)]
            picked = jnp.dot(block, hot, preferred_element_type=jnp.float32)
            for part in range(per_phase):
                rows[which, pl.ds(part * pitch, RADIX), :] = picked[part * RADIX : (part + 1) * RADIX, :]
            for phase in range(RADIX):
                span = pl.ds(phase * per_phase, per_phase)
                taken = rows[which, pl.ds(phase, per_phase, stride=pitch), :] * keep[span, :]
                out_ref[span, :] = taken.astype(jnp.bfloat16)


def compact_paired(frames, frame_valid, valid_count, block_map):
    frame_dev, pixel_count = frames.shape
    tile_count, tile_pix = block_map.shape
    slots = tile_pix // 2
    group = 4
    steps = tile_count // group
    place = pl.BlockSpec(memory_space=pl.ANY)
    return pl.pallas_call(
        functools.partial(paired_kernel, group),
        name="compact",
        out_shape=[jax.ShapeDtypeStruct((frame_dev, slots), jnp.bfloat16)] * tile_count,
        in_specs=[place] * 4,
        out_specs=[pl.BlockSpec(memory_space=pltpu.VMEM)] * tile_count,
        scratch_shapes=[
            pltpu.VMEM((steps, frame_dev, group * tile_pix), jnp.bfloat16),
            pltpu.VMEM((frame_dev, slots), jnp.float32),
            pltpu.VMEM((group, frame_dev // RADIX * (RADIX + 1) + 7, slots), jnp.float32),
            pltpu.SMEM((tile_count,), jnp.int32),
            pltpu.VMEM((1, frame_dev), jnp.int32),
            pltpu.VMEM((tile_count, tile_pix), jnp.int32),
            pltpu.SemaphoreType.DMA((steps,)),
            pltpu.SemaphoreType.DMA((3,)),
        ],
        compiler_params=pltpu.CompilerParams(vmem_limit_bytes=16 * 2**20),
    )(
        pltpu.with_memory_space_constraint(valid_count, pltpu.HBM),
        pltpu.with_memory_space_constraint(frame_valid.reshape(1, frame_dev), pltpu.HBM),
        pltpu.with_memory_space_constraint(block_map, pltpu.HBM),
        pltpu.with_memory_space_constraint(frames, pltpu.HBM),
    )


def turn_kernel(order, position_ref, table_ref, out_ref):
    per_phase = table_ref.shape[0] // len(order)
    for place, which in enumerate(order):
        source = jnp.bitwise_xor(position_ref[0], which)
        rows = pl.ds(pl.multiple_of(source * per_phase, per_phase), per_phase)
        out_ref[pl.ds(place * per_phase, per_phase), :] = table_ref[rows, :]


def turn_table(table, position, order):
    whole = pl.BlockSpec(memory_space=pltpu.VMEM)
    return pl.pallas_call(
        functools.partial(turn_kernel, order),
        name="turn",
        out_shape=jax.ShapeDtypeStruct(table.shape, table.dtype),
        in_specs=[pl.BlockSpec(memory_space=pltpu.SMEM), whole],
        out_specs=whole,
        compiler_params=pltpu.CompilerParams(vmem_limit_bytes=16 * 2**20),
    )(jnp.full((1,), position, jnp.int32), table)


def rotate(real, imag, cos, sin):
    return real * cos - imag * sin, real * sin + imag * cos


def four_point(values):
    (r0, i0), (r1, i1), (r2, i2), (r3, i3) = values
    er, ei, fr, fi = r0 + r2, i0 + i2, r0 - r2, i0 - i2
    gr, gi, hr, hi = r1 + r3, i1 + i3, r1 - r3, i1 - i3
    return [(er + gr, ei + gi), (fr + hi, fi - hr), (er - gr, ei - gi), (fr - hi, fi + hr)]


def sixteen_point_low(values):
    inner = [four_point([values[4 * n + m] for n in range(4)]) for m in range(4)]
    low = [None] * 8
    for k in range(4):
        parts = []
        for m in range(4):
            real, imag = inner[m][k]
            turn = m * k % 16
            if turn == 0:
                parts.append((real, imag))
            elif turn == 4:
                parts.append((imag, -real))
            else:
                angle = -2.0 * math.pi * turn / 16
                parts.append(rotate(real, imag, math.cos(angle), math.sin(angle)))
        (r0, i0), (r1, i1), (r2, i2), (r3, i3) = parts
        low[k] = ((r0 + r2) + (r1 + r3), (i0 + i2) + (i1 + i3))
        low[k + 4] = ((r0 - r2) + (i1 - i3), (i0 - i2) - (r1 - r3))
    return low


def transform_kernel(blocks, send_ref, table_ref, twiddle_ref, *rest):
    frames, own_ref = rest[:blocks], rest[blocks]
    edges, (phases, spread) = rest[blocks + 1 : -2], rest[-2:]
    slots = own_ref.shape[0] - 1
    rows = own_ref.shape[1]
    pitch = rows + 1
    half = rows // 2
    inner = table_ref.shape[0]
    edge = ROWS * REACH
    for phase in range(RADIX):
        if blocks > 1:
            per_phase = inner // blocks
            span = slice(phase * per_phase, (phase + 1) * per_phase)
            block = jnp.concatenate([ref[span, :] for ref in frames], axis=0)
        elif frames[0].shape[0] != RADIX:
            per_phase = frames[0].shape[1] // RADIX
            block = frames[0][:, phase * per_phase : (phase + 1) * per_phase, :].reshape(inner, slots)
        else:
            block = frames[0][phase].reshape(inner, slots)
        phases[phase] = lax.dot_general(
            block, table_ref[...], (((0,), (0,)), ((), ())), preferred_element_type=jnp.float32
        )
    groups = (send_ref[2 * (edge + 1)] + 7) // 8
    chunks = inner // LANES

    def one_group(group, carry):
        first = pl.multiple_of(group * 8, 8)
        for chunk in range(chunks):
            lanes = pl.ds(chunk * LANES, LANES)
            values = []
            for phase in range(RADIX):
                real = phases[phase, pl.ds(first, 8), lanes]
                imag = phases[phase, pl.ds(first, 8), pl.ds(inner + chunk * LANES, LANES)]
                if phase > 0:
                    real, imag = rotate(real, imag, twiddle_ref[phase, 0, :, lanes], twiddle_ref[phase, 1, :, lanes])
                values.append((real, imag))
            for high, (real, imag) in enumerate(sixteen_point_low(values)):
                at = first * pitch + high * chunks + chunk
                spread[pl.ds(at, 8, stride=pitch), :] = real
                spread[pl.ds(at + half, 8, stride=pitch), :] = imag
        return carry

    lax.fori_loop(0, groups, one_group, 0)

    def eight_slots(group, carry):
        for slot in range(8):
            slot = group * 8 + slot
            own_ref[slot] = spread[pl.ds(slot * pitch, rows), :].astype(jnp.bfloat16)
        return carry

    lax.fori_loop(0, groups, eight_slots, 0)
    own_ref[slots] = jnp.zeros((rows, LANES), jnp.bfloat16)
    nears, fars = edges[:2], edges[2:]
    bounds = [0] + [ref.shape[0] for ref in fars[:-1]]
    for low, high in zip(bounds[:-1], bounds[1:]):

        def one_edge(spot, carry, high=high):
            nears[0][spot] = own_ref[send_ref[spot]]
            block = own_ref[send_ref[edge + 1 + spot]]
            for ref in fars[:-1]:
                if ref.shape[0] >= high:
                    ref[spot] = block
            return carry

        lax.fori_loop(low, high, one_edge, 0, unroll=4)

    def one_rest(spot, carry):
        nears[1][spot] = own_ref[send_ref[bounds[-1] + spot]]
        fars[-1][spot] = own_ref[send_ref[edge + 1 + bounds[-1] + spot]]
        return carry

    lax.fori_loop(0, edge - bounds[-1], one_rest, 0, unroll=4)


def transform(send, table, twiddle, tile_frames, slots, frames_len):
    inner = frames_len // RADIX
    rows = frames_len // LANES
    edge = ROWS * REACH
    sizes = [CAPS[-1], edge - CAPS[-1], *CAPS, edge - CAPS[-1]]
    whole = pl.BlockSpec(memory_space=pltpu.VMEM)
    return pl.pallas_call(
        functools.partial(transform_kernel, len(tile_frames)),
        name="transform",
        out_shape=(
            jax.ShapeDtypeStruct((slots + 1, rows, LANES), jnp.bfloat16),
            *[jax.ShapeDtypeStruct((size, rows, LANES), jnp.bfloat16) for size in sizes],
        ),
        in_specs=[pl.BlockSpec(memory_space=pltpu.SMEM)] + [whole] * (2 + len(tile_frames)),
        out_specs=(whole,) * (1 + len(sizes)),
        scratch_shapes=[
            pltpu.VMEM((RADIX, slots, 2 * inner), jnp.float32),
            pltpu.VMEM((slots * (rows + 1) + 7, LANES), jnp.float32),
        ],
        compiler_params=pltpu.CompilerParams(vmem_limit_bytes=24 * 2**20),
    )(send, table, twiddle, *tile_frames)


def unpacked(code):
    return code % PART, code // PART % PART, code // PART // PART


def cross_terms(first, second):
    half = first.shape[0] // 2
    first = first.astype(jnp.float32)
    second = second.astype(jnp.float32)
    own_real, own_imag = first[:half], first[half:]
    real, imag = second[:half], second[half:]
    return own_real * real + own_imag * imag, own_imag * real - own_real * imag


def inside_kernel(place_ref, head_ref, list_ref, scale_ref, own_ref, near_ref, result, *totals):
    slots, rows = own_ref.shape[0] - 1, own_ref.shape[1]
    half = rows // 2
    offsets = len(totals)
    for total in totals:
        total[...] = jnp.zeros(total.shape, jnp.float32)

    def one_slot(slot, carry):
        pixel = place_ref[OFFSETS + 2, slot]
        column = pixel % totals[0].shape[0]
        own = own_ref[slot]
        for j, total in enumerate(totals):
            real, imag = cross_terms(own, own_ref[jnp.minimum(place_ref[j, pixel], slots)])
            total[column, :half] += real
            total[column, half:] += imag
        return carry

    lax.fori_loop(0, head_ref[0], one_slot, 0)
    for column in range(totals[0].shape[0]):
        for j, total in enumerate(totals):
            at = column * offsets + j
            scaling = scale_ref[j, column]
            result[at, pl.ds(0, half, stride=2), :] = total[column, :half] * scaling
            result[at, pl.ds(1, half, stride=2), :] = total[column, half:] * scaling

    near_row = head_ref[4]

    def one_pair(pair, carry):
        slot, other, at = unpacked(list_ref[near_row, pair])
        real, imag = cross_terms(own_ref[slot], near_ref[other - slots])
        scaling = scale_ref[at % offsets, at // offsets]
        result[at, pl.ds(0, half, stride=2), :] += real * scaling
        result[at, pl.ds(1, half, stride=2), :] += imag * scaling
        return carry

    lax.fori_loop(0, head_ref[1], one_pair, 0)


def inside(places, head, near_pairs, scale, own, near, tile_width, offsets):
    rows = own.shape[1]
    small = pl.BlockSpec(memory_space=pltpu.SMEM)
    whole = pl.BlockSpec(memory_space=pltpu.VMEM)
    return pl.pallas_call(
        inside_kernel,
        name="inside",
        out_shape=jax.ShapeDtypeStruct((tile_width * offsets, rows, LANES), jnp.float32),
        in_specs=[small] * 4 + [whole] * 2,
        out_specs=whole,
        scratch_shapes=[pltpu.VMEM((tile_width, rows, LANES), jnp.float32)] * offsets,
        compiler_params=pltpu.CompilerParams(vmem_limit_bytes=16 * 2**20),
        cost_estimate=pl.CostEstimate(flops=60_000_000, bytes_accessed=4_000_000, transcendentals=0),
    )(places, head, near_pairs, scale, own, near)


def across_kernel(head_ref, list_ref, scale_ref, own_ref, far_ref, part_ref, out_hbm, result, sem, inner_sem, *totals):
    slots, rows = own_ref.shape[0] - 1, own_ref.shape[1]
    half = rows // 2
    first_far = slots + ROWS * REACH
    spots = part_ref.shape[0]
    offsets = scale_ref.shape[0] // 2
    base = head_ref[2]
    border = REACH * offsets
    odd = head_ref[5]
    safe = pl.ds(jnp.where(odd == 1, 0, border), spots - border)
    inner = pltpu.make_async_copy(part_ref.at[safe], out_hbm.at[safe], inner_sem.at[0])
    inner.start()
    others = []
    for column in range(REACH):
        kept = pl.ds(base + column * offsets + jnp.where(odd == 1, 2, -2), 2)
        others.append(pltpu.make_async_copy(part_ref.at[kept], out_hbm.at[kept], inner_sem.at[1 + column]))
        others[-1].start()
    for total in totals:
        total[...] = jnp.zeros(total.shape, jnp.float32)
    far_row = head_ref[5]

    def some_pairs(group, carry):
        for which, total in enumerate(totals):
            slot, other, at = unpacked(list_ref[far_row, group * len(totals) + which])
            spot = (at - base) // offsets * 2 + (at - base) % offsets
            real, imag = cross_terms(own_ref[slot], far_ref[other - first_far])
            total[spot, :half] += real
            total[spot, half:] += imag
        return carry

    pairs = head_ref[3]
    lax.fori_loop(0, (pairs + len(totals) - 1) // len(totals), some_pairs, 0)
    copies = []
    for column in range(REACH):
        for j in range(2):
            spot = 2 * column + j
            at = base + column * offsets + j
            scaling = scale_ref[at % offsets, at // offsets]
            total = totals[0][spot]
            for other in totals[1:]:
                total = total + other[spot]
            total = total * scaling
            result[spot, pl.ds(0, half, stride=2), :] = part_ref[at, pl.ds(0, half, stride=2), :] + total[:half]
            result[spot, pl.ds(1, half, stride=2), :] = part_ref[at, pl.ds(1, half, stride=2), :] + total[half:]
        copies.append(
            pltpu.make_async_copy(
                result.at[pl.ds(2 * column, 2)], out_hbm.at[pl.ds(base + column * offsets, 2)], sem.at[column]
            )
        )
        copies[-1].start()
    for copy in [inner, *others, *copies]:
        copy.wait()


def across(head, far_pairs, scale, own, far, part):
    rows = own.shape[1]
    small = pl.BlockSpec(memory_space=pltpu.SMEM)
    whole = pl.BlockSpec(memory_space=pltpu.VMEM)
    return pl.pallas_call(
        across_kernel,
        name="across",
        out_shape=pltpu.HBM(part.shape, part.dtype),
        in_specs=[small, small, small, whole, whole, whole],
        out_specs=pl.BlockSpec(memory_space=pl.ANY),
        scratch_shapes=[
            pltpu.VMEM((2 * REACH, rows, LANES), jnp.float32),
            pltpu.SemaphoreType.DMA((REACH,)),
            pltpu.SemaphoreType.DMA((1 + REACH,)),
        ]
        + [pltpu.VMEM((2 * REACH, rows, LANES), jnp.float32)] * LANES_OF_PAIRS,
        compiler_params=pltpu.CompilerParams(vmem_limit_bytes=16 * 2**20),
    )(head, far_pairs, scale, own, far, part)


def plan_kernel(offset_ref, position_ref, count_ref, map_ref, table_ref, scale_ref, level_ref):
    tile_count, pixels = map_ref.shape
    slots = pixels // 2
    tile_width = pixels // ROWS
    edge = ROWS * REACH
    empty = slots + 2 * edge
    position = position_ref[0]
    offsets = [(offset_ref[j, 0], offset_ref[j, 1]) for j in range(offset_ref.shape[0])]
    held = jnp.where(
        lax.broadcasted_iota(jnp.int32, (tile_count, slots), 1) < count_ref[...], map_ref[:, :slots], -1
    )
    pixel = lax.broadcasted_iota(jnp.int32, (tile_count, pixels), 1)
    tile = lax.broadcasted_iota(jnp.int32, (tile_count, pixels), 0)
    row = pixel // tile_width
    column = pixel % tile_width
    found = jnp.zeros((tile_count, pixels), jnp.int32)
    for slot in range(slots):
        found = jnp.where(held[:, slot : slot + 1] == pixel, slot + 1, found)
    valid = jnp.where(found > 0, 1, 0)
    left_valid = jnp.where(tile > 0, pltpu.roll(valid, 1, 0), 0)
    right_valid = jnp.where(tile < tile_count - 1, pltpu.roll(valid, tile_count - 1, 0), 0)

    def turned(values, shift):
        return pltpu.roll(values, lax.rem(shift + 2 * pixels, pixels), 1)

    for_left = jnp.zeros((tile_count, pixels), jnp.int32)
    for_right = jnp.zeros((tile_count, pixels), jnp.int32)
    for down, across_by in offsets:
        shift = down * tile_width + across_by
        inside_rows = (row >= down) & (row < ROWS + down)
        partner = turned(left_valid, shift - tile_width)
        for_left = jnp.where(inside_rows & (column < across_by), jnp.maximum(for_left, partner), for_left)
        partner = turned(right_valid, shift + tile_width)
        for_right = jnp.where(
            inside_rows & (column >= tile_width + across_by), jnp.maximum(for_right, partner), for_right
        )
    before = jnp.where(
        lax.broadcasted_iota(jnp.int32, (pixels, pixels), 0) <= lax.broadcasted_iota(jnp.int32, (pixels, pixels), 1),
        1.0,
        0.0,
    ).astype(jnp.bfloat16)

    def numbered(needed):
        needed = (needed * valid).astype(jnp.float32)
        ranks = jnp.dot(needed.astype(jnp.bfloat16), before, preferred_element_type=jnp.float32) * needed
        return ranks.astype(jnp.int32), jnp.max(ranks)

    left_rank, left_most = numbered(for_left)
    right_rank, right_most = numbered(for_right)
    most = jnp.maximum(left_most, right_most)
    sent_far = jnp.max(jnp.where(tile % 2 == 0, left_rank, right_rank).astype(jnp.float32))
    level = sum([jnp.where(sent_far <= cap, 0, 1) for cap in CAPS])
    level_ref[0] = jnp.where(most <= CAPS[-1], level, len(CAPS))

    def chosen(values, which):
        picked = jnp.sum(jnp.where(tile == which, values, 0), axis=0, keepdims=True)
        return jnp.broadcast_to(picked, (8, pixels))

    odd = lax.rem(position, 2)
    row, column = row[:8], column[:8]
    own = chosen(found, position)
    right = chosen(left_rank, position + 1)
    left = chosen(right_rank, position - 1)
    own_place = jnp.where(own > 0, own - 1, empty)
    right_place = jnp.where(right > 0, slots + odd * edge - 1 + right, empty)
    left_place = jnp.where(left > 0, slots + (1 - odd) * edge - 1 + left, empty)
    selector = jnp.where(
        lax.broadcasted_iota(jnp.int32, (pixels, LANES), 0) % tile_width
        == lax.broadcasted_iota(jnp.int32, (pixels, LANES), 1),
        1.0,
        0.0,
    ).astype(jnp.bfloat16)
    spot = lax.broadcasted_iota(jnp.int32, (8, pixels), 0)
    seen = jnp.zeros((8, pixels), jnp.float32)
    table = jnp.zeros((8, pixels), jnp.int32)
    codes = jnp.where(spot == len(offsets), own - 1, -1)
    for j, (down, across_by) in enumerate(offsets):
        shift = down * tile_width + across_by
        other = turned(own_place, -shift)
        other = jnp.where(column + across_by < 0, turned(left_place, -shift - tile_width), other)
        other = jnp.where(column + across_by >= tile_width, turned(right_place, tile_width - shift), other)
        other = jnp.where((row + down >= 0) & (row + down < ROWS), other, empty)
        seen = jnp.where((spot == j) & (own > 0) & (other < empty), 1.0, seen)
        table = jnp.where(spot == j, other, table)
        code = ((column * len(offsets) + j) * PART + other) * PART + own - 1
        crossing = (spot == j) & (own > 0) & (other >= slots) & (other < empty)
        codes = jnp.where(crossing, code, codes)
    own_left = chosen(left_rank, position)
    own_right = chosen(right_rank, position)
    near = jnp.where(odd == 1, own_left, own_right)
    far = jnp.where(odd == 1, own_right, own_left)
    table = jnp.where(spot == len(offsets), jnp.where(near > 0, near - 1, edge), table)
    table = jnp.where(spot == len(offsets) + 1, jnp.where(far > 0, far - 1, edge), table)
    wide = jnp.concatenate([held, held], axis=1)
    table_ref[:8, :] = jnp.where(spot == len(offsets) + 2, chosen(wide, position), table)
    table_ref[8:, :] = codes
    pairs = jnp.dot(seen.astype(jnp.bfloat16), selector, preferred_element_type=jnp.float32)
    scale_ref[...] = 1.0 / jnp.maximum(pairs, 1.0)


def listing_kernel(table_ref, count_ref, position_ref, head_ref, send_ref, list_ref):
    slots = table_ref.shape[1] // 2
    tile_width = table_ref.shape[1] // ROWS
    edge = ROWS * REACH
    position = position_ref[0]
    odd = lax.rem(position, 2)

    def clear(spot, carry):
        send_ref[spot] = 0
        return carry

    lax.fori_loop(0, 2 * (edge + 1), clear, 0, unroll=26)

    def one_row(row, listed):
        listed = list(listed)
        for side, first_column in enumerate((0, tile_width - REACH)):
            for column in range(first_column, first_column + REACH):
                pixel = row * tile_width + column
                slot = table_ref[8 + OFFSETS, pixel]
                send_ref[table_ref[OFFSETS, pixel]] = slot
                send_ref[edge + 1 + table_ref[OFFSETS + 1, pixel]] = slot
                for j in range(OFFSETS // 2):
                    code = table_ref[8 + (1 - side) * (OFFSETS // 2) + j, pixel]
                    list_ref[side, listed[side]] = code
                    listed[side] = listed[side] + jnp.where(code >= 0, 1, 0)
        return tuple(listed)

    left, right = lax.fori_loop(0, ROWS, one_row, (0, 0))
    base = jnp.where(odd == 1, (tile_width - REACH) * OFFSETS, OFFSETS // 2)
    close = jnp.where(odd == 1, left, right)
    distant = jnp.where(odd == 1, right, left)
    for spare in range(LANES_OF_PAIRS - 1):
        list_ref[odd, distant + spare] = (base * PART + slots + edge) * PART + slots
    count = count_ref[position]
    send_ref[2 * (edge + 1)] = count
    for spot, value in enumerate((count, close, base, distant, 1 - odd, odd)):
        head_ref[spot] = value


def plan(valid_count, block_map, offsets, position):
    tile_count, pixels = block_map.shape
    slots = pixels // 2
    small = pl.BlockSpec(memory_space=pltpu.SMEM)
    whole = pl.BlockSpec(memory_space=pltpu.VMEM)
    position = jnp.full((1,), position, jnp.int32)
    table, scale, level = pl.pallas_call(
        plan_kernel,
        name="plan",
        out_shape=(
            jax.ShapeDtypeStruct((16, pixels), jnp.int32),
            jax.ShapeDtypeStruct((8, LANES), jnp.float32),
            jax.ShapeDtypeStruct((1,), jnp.int32),
        ),
        in_specs=[small, small, whole, whole],
        out_specs=(whole, whole, small),
        compiler_params=pltpu.CompilerParams(vmem_limit_bytes=16 * 2**20),
    )(offsets, position, valid_count.reshape(tile_count, 1), block_map)
    head, send, listed = pl.pallas_call(
        listing_kernel,
        name="listing",
        out_shape=(
            jax.ShapeDtypeStruct((6,), jnp.int32),
            jax.ShapeDtypeStruct((2 * (ROWS * REACH + 1) + 1,), jnp.int32),
            jax.ShapeDtypeStruct((2, ROWS * REACH * OFFSETS // 2 + LANES_OF_PAIRS), jnp.int32),
        ),
        in_specs=[small, small, small],
        out_specs=(small,) * 3,
        compiler_params=pltpu.CompilerParams(vmem_limit_bytes=16 * 2**20),
    )(table, valid_count, position)
    return table, scale, level[0], head, send, listed


def finish(level, near_pairs, far_pairs, tile_width, offsets, operands):
    places, head, scale, listed, own, *edges = operands
    nears, fars = edges[:2], edges[2:]
    if level < len(CAPS):
        near, far = nears[0], fars[level]
    else:
        near, far = jnp.concatenate(nears), jnp.concatenate(fars[-2:])
    far = lax.ppermute(far, "tm", far_pairs)
    near = lax.ppermute(near, "tm", near_pairs)
    part = inside(places, head, listed, scale, own, near, tile_width, offsets)
    result = across(head, listed, scale, own, far, part)
    groups = result.shape[1] // 2
    result = result.reshape(tile_width, offsets, groups, 2, LANES)
    return result.transpose(0, 1, 3, 2, 4).reshape(tile_width, offsets, 2, groups * LANES)


def per_device(frames, frame_valid, valid_count, block_map, offsets):
    devices = lax.axis_size("tm")
    position = lax.axis_index("tm")
    frame_dev = frames.shape[0]
    frames_len = frame_dev * devices
    tile_pix = block_map.shape[1]
    slots = tile_pix // 2
    tile_width = tile_pix // ROWS
    table, twiddle = dft_tables(frames_len)
    per_phase = frame_dev // RADIX
    if devices == PAIRED and per_phase % 16 == 0:
        order = send_order(devices)
        sent = compact_paired(frames, frame_valid, valid_count, block_map)
        pairs = [[(i, i ^ which) for i in range(devices)] for which in order]
        tile_frames = [lax.ppermute(sent[which], "tm", pair) for which, pair in zip(order, pairs)] + [sent[0]]
        table = turn_table(table, position, order + [0])
    else:
        sent = compact(frames, frame_valid, valid_count, block_map)
        received = lax.all_to_all(sent, "tm", split_axis=0, concat_axis=0, tiled=True)
        if per_phase % 16 != 0 or devices == RADIX:
            received = received.reshape(devices, RADIX, per_phase, slots)
            received = received.transpose(1, 0, 2, 3).reshape(RADIX, frames_len // RADIX, slots)
        tile_frames = [received]
    places, scale, level, head, send, listed = plan(valid_count, block_map, offsets, position)
    outs = transform(send, table, twiddle, tile_frames, slots, frames_len)
    far_pairs = [(i, i + 1) for i in range(1, devices - 1, 2)] + [(i + 1, i) for i in range(1, devices - 1, 2)]
    near_pairs = [(i, i + 1) for i in range(0, devices - 1, 2)] + [(i + 1, i) for i in range(0, devices - 1, 2)]
    branches = [
        functools.partial(finish, which, near_pairs, far_pairs, tile_width, offsets.shape[0])
        for which in range(len(CAPS) + 1)
    ]
    return lax.switch(level, branches, (places, head, scale, listed, *outs))


def solution(mesh):
    return jax.shard_map(
        per_device,
        mesh=mesh,
        in_specs=(P("tm", "groups"), P(("groups", "tm")), P("groups"), P("groups", None), P()),
        out_specs=P(("groups", "tm"), None, None, None),
        check_vma=False,
    )
```
